32 devices in a mesh: seq: 16 (over z, y, core), mp: 2 (over x).
Axes of the slice: x: 2, y: 2, z: 4, core: 2. Of those that a mesh axis runs over, the one named last changes fastest.
Arguments:
- shared_qk: bfloat16 [2048, 4096], P('seq', 'mp'), may hold values from -40 to 40
- values: bfloat16 [2048, 4096], P('seq', 'mp'), may hold values from -6 to 6
- buckets: int32 [2048, 32], P('seq', 'mp'), may hold values from 0 to 15, as said below
- counts: int32 [16, 32, 16], P(None, 'mp'), may hold values from 0 to 16, as said below
- w_out: bfloat16 [4096, 4096], P('mp'), may hold values from -0.09375 to 0.09375
Outputs:
- projected: bfloat16 [2048, 4096], P('seq', 'mp')
The draws below stay inside these ranges and needn't reach their ends.
Inputs may be any that keep to these rules, and one draw needn't show every extreme that they name: `buckets`: in each head at most 16 tokens among rows d * 128 to (d + 1) * 128 - 1 name one bucket, and in each head one bucket is named by exactly 16 tokens of every such group of rows. counts[d, h, b] is the number of rows among d * 128 to (d + 1) * 128 - 1 whose bucket in head h is b.
All inputs are finite; a program needn't handle non-finite values.
Results may differ from the reference program's by a relative error of at most 0.0057.
Values may be sent and summed in bfloat16 or wider, within the bound.
No kernel may reach another device: no remote copies, remote signals or barrier semaphores. Data moves between devices by JAX's collectives and lax.ppermute only.
A program may use at most 64 MiB of HBM per device.

```python
import math
import jax
import jax.numpy as jnp
from jax import lax

D = 4096
H = 32
DH = 128
BLOCK = 256
TOK_DEV = 128
TOKENS = 2048
NBK = 16
CAP = 16
SLOTS = 256


def routing_tables(key):
    seeded = jax.random.fold_in(key, 1234)
    key_bias, key_full, key_jitter, key_perm = jax.random.split(seeded, 4)
    tickets = NBK * CAP
    bucket_range = jnp.arange(NBK)
    bucket_bias = jax.random.randint(key_bias, (H, NBK), 0, 2048)
    full_bucket = jax.random.randint(key_full, (H,), 0, NBK)
    bucket_bias = jnp.where(bucket_range[None, :] == full_bucket[:, None], 16384, bucket_bias)
    ticket_bucket = jnp.arange(tickets) // CAP
    jitter = jax.random.randint(key_jitter, (NBK, H, tickets), 0, 1024)
    ticket_score = (bucket_bias[:, ticket_bucket][None] + jitter) * 4096 + jnp.arange(tickets)[None, None, :]
    unused_scores, chosen = lax.top_k(ticket_score, TOK_DEV)
    chosen_bucket = (chosen // CAP).astype(jnp.int32).reshape(NBK * H, TOK_DEV)
    counts = jax.vmap(lambda row: jnp.bincount(row, length=NBK))(chosen_bucket).reshape(NBK, H, NBK)
    perm_keys = jax.random.split(key_perm, NBK * H)
    perms = jax.vmap(lambda single: jax.random.permutation(single, TOK_DEV))(perm_keys)
    shuffled = jnp.take_along_axis(chosen_bucket, perms, axis=1).reshape(NBK, H, TOK_DEV)
    buckets = jnp.transpose(shuffled, (0, 2, 1)).reshape(TOKENS, H)
    return (buckets.astype(jnp.int32), counts.astype(jnp.int32))


def draw_buckets(key, part):
    return routing_tables(key)[0]


def draw_counts(key, part):
    return routing_tables(key)[1]


def draw_shared_qk(key, part):
    key_base = jax.random.fold_in(jax.random.fold_in(key, 77), 0)
    normal_part = jax.random.normal(key_base, (TOKENS, H, DH), jnp.float32)
    return jnp.clip(normal_part, -40.0, 40.0).reshape(TOKENS, H * DH).astype(jnp.bfloat16)


def block_levels(rng, extent, cuts, smallest, top_value):
    factor_of, own = 1.0, jax.random.fold_in(rng, 6)
    for axis_at, shards_of in cuts:
        heights = jnp.exp(jax.random.uniform(jax.random.fold_in(own, axis_at), (shards_of,), jnp.float32, smallest / len(cuts), top_value / len(cuts)))
        factor_of = factor_of * jnp.repeat(heights, extent[axis_at] // shards_of).reshape([-1 if axis == axis_at else 1 for axis in range(len(extent))])
    return factor_of


def gaussian(own_key, shape, width, bound, cuts=(), held_as=jnp.bfloat16):
    drawn = jax.random.normal(own_key, shape, jnp.float32) * width
    if len(cuts) > 0:
        drawn = block_levels(own_key, shape, cuts, -0.22, 0.18) * drawn
    return jnp.clip(drawn, min=-bound, max=bound).astype(held_as)


def setup_inputs(seed: int = 0) -> dict:
    arg_keys = jax.random.split(jax.random.key(seed), 6)
    shared_qk = draw_shared_qk(jax.random.fold_in(arg_keys[5], 71), 0)
    values = gaussian(arg_keys[1], (TOKENS, H * DH), 1.0, 6.0, ((0, 16), (1, 2)))
    buckets = draw_buckets(jax.random.fold_in(arg_keys[5], 71), 0)
    counts = draw_counts(jax.random.fold_in(arg_keys[5], 71), 0)
    w_out = gaussian(arg_keys[4], (H * DH, D), (H * DH) ** -0.5, 0.09375, ((0, 2),))
    return {"shared_qk": shared_qk, "values": values, "buckets": buckets, "counts": counts, "w_out": w_out}


SELF_SCORE = -100000.0

def block_attention(queries, window, window_live):
    head_dim = queries.shape[-1]
    block_rows = queries.shape[-2]
    key_rows = window[..., :head_dim].astype(jnp.float32)
    value_rows = window[..., head_dim:].astype(jnp.float32)
    scores = jnp.einsum('cqd,ckd->cqk', queries.astype(jnp.float32), key_rows) * (1.0 / math.sqrt(head_dim))
    query_place = jnp.arange(block_rows)[:, None] + block_rows
    key_place = jnp.arange(2 * block_rows)[None, :]
    itself = query_place == key_place
    scores = jnp.where(itself[None], SELF_SCORE, scores)
    allowed = window_live[:, None, :] | itself[None]
    row_max = lax.optimization_barrier(jnp.max(jnp.where(allowed, scores, -1e+30), axis=-1, keepdims=True))
    exp_terms = jnp.where(allowed, jnp.exp(scores - row_max), 0.0)
    weights = (exp_terms / lax.optimization_barrier(jnp.sum(exp_terms, axis=-1, keepdims=True))).astype(jnp.bfloat16)
    attended = jnp.einsum('cqk,ckd->cqd', weights.astype(jnp.float32), value_rows)
    return attended.astype(jnp.bfloat16)

def attend_head(qk_head, value_head, bucket_head, size_head):
    positions = jnp.arange(TOKENS).astype(jnp.int32)
    token_order = jnp.argsort(bucket_head * TOKENS + positions).astype(jnp.int32)
    sorted_bucket = bucket_head[token_order]
    seg_starts = (jnp.cumsum(size_head) - size_head).astype(jnp.int32)
    sorted_rank = (positions - seg_starts[sorted_bucket]).astype(jnp.int32)
    slot_index = (sorted_bucket * SLOTS + sorted_rank).astype(jnp.int32)
    packed = jnp.concatenate([qk_head, value_head], axis=1)
    layout = jnp.zeros((NBK * SLOTS, 2 * DH), packed.dtype).at[slot_index].set(packed[token_order])
    layout = layout.reshape(NBK, SLOTS, 2 * DH)
    live = jnp.arange(SLOTS)[None, :] < size_head[:, None]
    rank_index = (size_head[:, None] - BLOCK + jnp.arange(BLOCK)[None, :]).astype(jnp.int32)
    tail_live = rank_index >= 0
    seg_range = jnp.arange(NBK)[:, None]
    tail_rows = layout[seg_range, jnp.maximum(rank_index, 0)]
    tail_rows = jnp.where(tail_live[..., None], tail_rows, jnp.zeros((), tail_rows.dtype))
    prev_rows = jnp.roll(tail_rows, 1, axis=0)
    prev_live = jnp.roll(tail_live, 1, axis=0)
    keys_all = jnp.concatenate([prev_rows, layout], axis=1)
    live_all = jnp.concatenate([prev_live, live], axis=1)
    block_count = SLOTS // BLOCK
    window = jnp.concatenate([keys_all[:, :SLOTS].reshape(NBK, block_count, BLOCK, 2 * DH), keys_all[:, BLOCK:].reshape(NBK, block_count, BLOCK, 2 * DH)], axis=2)
    window_live = jnp.concatenate([live_all[:, :SLOTS].reshape(NBK, block_count, BLOCK), live_all[:, BLOCK:].reshape(NBK, block_count, BLOCK)], axis=2)
    queries = layout[..., :DH].reshape(NBK * block_count, BLOCK, DH)
    attended = block_attention(queries, window.reshape(NBK * block_count, 2 * BLOCK, 2 * DH), window_live.reshape(NBK * block_count, 2 * BLOCK))
    out_layout = attended.reshape(NBK * SLOTS, DH)
    token_slot = jnp.zeros((TOKENS,), jnp.int32).at[token_order].set(slot_index)
    return out_layout[token_slot]

def reference(shared_qk, values, buckets, counts, w_out):
    qk_heads = jnp.transpose(shared_qk.reshape(TOKENS, H, DH), (1, 0, 2))
    value_heads = jnp.transpose(values.reshape(TOKENS, H, DH), (1, 0, 2))
    bucket_heads = buckets.T.astype(jnp.int32)
    sizes = lax.optimization_barrier(jnp.sum(counts, axis=0)).astype(jnp.int32)
    per_head = lax.map(lambda item: attend_head(item[0], item[1], item[2], item[3]), (qk_heads, value_heads, bucket_heads, sizes))
    attended = jnp.transpose(per_head, (1, 0, 2)).reshape(TOKENS, H * DH)
    projected = jnp.dot(attended.astype(jnp.float32), w_out.astype(jnp.float32), preferred_element_type=jnp.float32)
    return projected.astype(jnp.bfloat16)
```

```python
import functools
import math

import jax
import jax.numpy as jnp
from jax import lax
from jax.experimental import pallas as pl
from jax.experimental.pallas import tpu as pltpu
from jax.sharding import PartitionSpec as P

BLOCK = 256
MASKED = -1e30


SELF_SCORE = -100000.0


def passed_along(shard, axis, by):
    devices = lax.axis_size(axis)
    return lax.ppermute(shard, axis, [(i, (i + by) % devices) for i in range(devices)])


def block_attention(queries, window, window_live):
    head_dim = queries.shape[-1]
    block_rows = queries.shape[-2]
    key_rows = window[..., :head_dim]
    value_rows = window[..., head_dim:]
    scores = jnp.einsum("cqd,ckd->cqk", queries, key_rows, preferred_element_type=jnp.float32) * (
        1.0 / math.sqrt(head_dim)
    )
    query_place = jnp.arange(block_rows)[:, None] + block_rows
    key_place = jnp.arange(2 * block_rows)[None, :]
    itself = query_place == key_place
    scores = jnp.where(itself[None], SELF_SCORE, scores)
    allowed = window_live[:, None, :] | itself[None]
    row_max = jnp.max(jnp.where(allowed, scores, -1e30), axis=-1, keepdims=True)
    exp_terms = jnp.where(allowed, jnp.exp(scores - row_max), 0.0)
    weights = (exp_terms / jnp.sum(exp_terms, axis=-1, keepdims=True)).astype(jnp.bfloat16)
    attended = jnp.einsum("cqk,ckd->cqd", weights, value_rows, preferred_element_type=jnp.float32)
    return attended.astype(jnp.bfloat16)


def owner_layout(received, column, slot_count):
    source_count = column.shape[0]
    head_count = column.shape[1]
    upto_count = jnp.cumsum(column, axis=0)
    before_count = upto_count - column
    bucket_total = upto_count[-1]
    slot_range = jnp.arange(slot_count)
    source_dev = jnp.sum(upto_count[:, :, None] <= slot_range[None, None, :], axis=0)
    source_dev = jnp.minimum(source_dev, source_count - 1)
    source_range = jnp.arange(source_count)
    source_start = jnp.sum(
        jnp.where(source_dev[None] == source_range[:, None, None], before_count[:, :, None], 0),
        axis=0,
    )
    entry_row = jnp.clip(slot_range[None, :] - source_start, 0, received.shape[2] - 1)
    head_range = jnp.arange(head_count)
    layout = received[source_dev, head_range[:, None], entry_row]
    live = slot_range[None, :] < bucket_total[:, None]
    layout = jnp.where(live[..., None], layout, jnp.zeros((), layout.dtype))
    return (layout, live, before_count, bucket_total)


def tail_live(bucket_total, block_rows):
    return bucket_total[:, None] - block_rows + jnp.arange(block_rows)[None, :] >= 0


def last_rows(layout, bucket_total, block_rows):
    rank_index = bucket_total[:, None] - block_rows + jnp.arange(block_rows)[None, :]
    head_range = jnp.arange(layout.shape[0])
    rows = layout[head_range[:, None], jnp.maximum(rank_index, 0)]
    return jnp.where((rank_index >= 0)[..., None], rows, jnp.zeros((), rows.dtype))


def local_by_bucket(shared_qk, values, buckets, counts, w_out):
    tok_rows = shared_qk.shape[0]
    head_count = buckets.shape[1]
    head_dim = shared_qk.shape[1] // head_count
    seq_count = lax.axis_size("seq")
    capacity = 2 * tok_rows // seq_count
    slot_count = seq_count * capacity
    block_rows = BLOCK
    block_count = slot_count // block_rows
    own_index = lax.axis_index("seq")
    prev_index = (own_index + seq_count - 1) % seq_count
    head_range = jnp.arange(head_count)
    bucket_heads = buckets.T
    positions = jnp.arange(tok_rows)
    earlier = positions[None, :] < positions[:, None]
    same_bucket = bucket_heads[:, :, None] == bucket_heads[:, None, :]
    within = jnp.sum(same_bucket & earlier[None], axis=2)
    own_counts = lax.dynamic_index_in_dim(counts, own_index, 0, keepdims=False)
    own_starts = jnp.cumsum(own_counts, axis=1) - own_counts
    bucket_range = jnp.arange(seq_count)
    one_hot = bucket_heads[:, :, None] == bucket_range[None, None, :]
    token_start = jnp.sum(jnp.where(one_hot, own_starts[:, None, :], 0), axis=2)
    sorted_pos = token_start + within
    token_order = jnp.sum(
        jnp.where(sorted_pos[:, :, None] == positions[None, None, :], positions[None, :, None], 0),
        axis=1,
    )
    slot_range = jnp.arange(capacity)
    send_index = own_starts.T[:, :, None] + slot_range[None, None, :]
    filled = slot_range[None, None, :] < own_counts.T[:, :, None]
    token_pick = token_order[head_range[None, :, None], jnp.minimum(send_index, tok_rows - 1)]
    packed = jnp.concatenate(
        [
            shared_qk.reshape(tok_rows, head_count, head_dim),
            values.reshape(tok_rows, head_count, head_dim),
        ],
        axis=2,
    )
    outgoing = packed[token_pick, head_range[None, :, None]]
    outgoing = jnp.where(filled[..., None], outgoing, jnp.zeros((), outgoing.dtype))
    own_column = lax.dynamic_index_in_dim(counts, own_index, 2, keepdims=False)
    prev_column = lax.dynamic_index_in_dim(counts, prev_index, 2, keepdims=False)
    prev_total = jnp.sum(prev_column, axis=0)
    received = lax.all_to_all(outgoing, "seq", split_axis=0, concat_axis=0, tiled=True)
    layout, live, before_count, bucket_total = owner_layout(received, own_column, slot_count)
    tail_rows = last_rows(layout, bucket_total, block_rows)
    prev_rows = passed_along(tail_rows, "seq", 1)
    prev_live = tail_live(prev_total, block_rows)
    keys_all = jnp.concatenate([prev_rows, layout], axis=1)
    live_all = jnp.concatenate([prev_live, live], axis=1)
    window = jnp.concatenate(
        [
            keys_all[:, :slot_count].reshape(head_count, block_count, block_rows, 2 * head_dim),
            keys_all[:, block_rows:].reshape(head_count, block_count, block_rows, 2 * head_dim),
        ],
        axis=2,
    )
    window_live = jnp.concatenate(
        [
            live_all[:, :slot_count].reshape(head_count, block_count, block_rows),
            live_all[:, block_rows:].reshape(head_count, block_count, block_rows),
        ],
        axis=2,
    )
    queries = layout[..., :head_dim].reshape(head_count, block_count, block_rows, head_dim)
    attended = lax.map(
        lambda per_head: block_attention(per_head[0], per_head[1], per_head[2]),
        (queries, window, window_live),
    )
    out_layout = attended.reshape(head_count, slot_count, head_dim)
    back_index = before_count[:, :, None] + slot_range[None, None, :]
    back_filled = slot_range[None, None, :] < own_column[:, :, None]
    back_rows = out_layout[head_range[None, :, None], jnp.minimum(back_index, slot_count - 1)]
    back_rows = jnp.where(back_filled[..., None], back_rows, jnp.zeros((), back_rows.dtype))
    returned = lax.all_to_all(back_rows, "seq", split_axis=0, concat_axis=0, tiled=True)
    token_out = returned[buckets, head_range[None, :], within.T]
    token_out = token_out.reshape(tok_rows, head_count * head_dim)
    partial_sum = jnp.dot(token_out, w_out, preferred_element_type=jnp.float32)
    projected = lax.psum_scatter(partial_sum, "mp", scatter_dimension=1, tiled=True)
    return projected.astype(jnp.bfloat16)


def weights_kernel(bucket_ref, qk_ref, out_ref, query_ref, key_ref, score_ref, *, bucket_count, query_rows):
    source_count, tok_rows = bucket_ref.shape
    head_dim = qk_ref.shape[1]
    token_count = qk_ref.shape[0]
    lanes = query_ref.shape[1] - head_dim
    lane = lax.broadcasted_iota(jnp.int32, (tok_rows, lanes), 1)
    query_ref[:, :head_dim] = qk_ref[...]
    key_ref[:, :head_dim] = qk_ref[...]
    for source in range(source_count):
        rows = slice(source * tok_rows, (source + 1) * tok_rows)
        row = bucket_ref[source : source + 1, :].astype(jnp.float32)
        bucket = jnp.broadcast_to(row, (lanes, tok_rows)).T.astype(jnp.int32)
        following = jnp.where(bucket == bucket_count - 1, 0, bucket + 1)
        own = lane == bucket
        query_ref[rows, head_dim:] = jnp.where(own, 1.0, 0.0).astype(query_ref.dtype)
        key_ref[rows, head_dim:] = jnp.where(own | (lane == following), 0.0, MASKED).astype(key_ref.dtype)
    scale = 1.0 / math.sqrt(head_dim)
    strip = 16

    def one_block(block, carry):
        start = pl.multiple_of(block * query_rows, query_rows)
        score_ref[...] = lax.dot_general(
            query_ref[pl.ds(start, query_rows), :],
            key_ref[...],
            (((1,), (1,)), ((), ())),
            preferred_element_type=jnp.float32,
        )
        square = (query_rows, query_rows)
        itself = lax.broadcasted_iota(jnp.int32, square, 0) == lax.broadcasted_iota(jnp.int32, square, 1)
        own_columns = score_ref[:, pl.ds(start, query_rows)]
        score_ref[:, pl.ds(start, query_rows)] = jnp.where(itself, SELF_SCORE / scale, own_columns)
        for at in range(0, query_rows, strip):
            scores = score_ref[at : at + strip, :]
            row_max = jnp.max(scores, axis=1, keepdims=True)
            exp_terms = jnp.exp((scores - row_max) * scale)
            inverse = 1.0 / jnp.sum(exp_terms, axis=1, keepdims=True)
            out_ref[pl.ds(start + at, strip), :] = (exp_terms * inverse).astype(out_ref.dtype)
        return carry

    lax.fori_loop(0, token_count // query_rows, one_block, 0)


def head_weights(bucket, qk, bucket_count):
    token_count, head_dim = qk.shape
    lanes = 128
    query_rows = min(256, token_count)
    return pl.pallas_call(
        functools.partial(weights_kernel, bucket_count=bucket_count, query_rows=query_rows),
        out_shape=jax.ShapeDtypeStruct((token_count, token_count), qk.dtype),
        scratch_shapes=[
            pltpu.VMEM((token_count, head_dim + lanes), qk.dtype),
            pltpu.VMEM((token_count, head_dim + lanes), qk.dtype),
            pltpu.VMEM((query_rows, token_count), jnp.float32),
        ],
        name="head_weights",
    )(bucket, qk)


def attend_kernel(weight_ref, value_ref, out_ref):
    out_ref[...] = jnp.dot(
        weight_ref[...], value_ref[...], preferred_element_type=jnp.float32
    ).astype(out_ref.dtype)


def head_attend(weights, value):
    token_count, head_dim = value.shape
    rows = min(512, token_count)
    return pl.pallas_call(
        attend_kernel,
        grid=(token_count // rows,),
        in_specs=[
            pl.BlockSpec((rows, token_count), lambda i: (i, 0)),
            pl.BlockSpec((token_count, head_dim), lambda i: (0, 0)),
        ],
        out_specs=pl.BlockSpec((rows, head_dim), lambda i: (i, 0)),
        out_shape=jax.ShapeDtypeStruct((token_count, head_dim), value.dtype),
        name="head_attend",
    )(weights, value)


def project_kernel(part_ref, token_ref, w_ref, out_ref, wide_ref):
    head_count, tok_rows, head_dim = token_ref.shape

    @pl.when(pl.program_id(0) == 0)
    def _():
        for head in range(head_count):
            wide_ref[:, head * head_dim : (head + 1) * head_dim] = token_ref[head]

    out_ref[...] = jnp.dot(
        wide_ref[...], w_ref[...], preferred_element_type=jnp.float32
    ).astype(out_ref.dtype)


def project_part(token_heads, w_out, part, part_count, dtype):
    head_count, tok_rows, head_dim = token_heads.shape
    depth, features = w_out.shape
    width = features // part_count
    columns = min(512, width)
    steps = width // columns
    return pl.pallas_call(
        project_kernel,
        grid_spec=pltpu.PrefetchScalarGridSpec(
            num_scalar_prefetch=1,
            grid=(steps,),
            in_specs=[
                pl.BlockSpec((head_count, tok_rows, head_dim), lambda j, part_ref: (0, 0, 0)),
                pl.BlockSpec((depth, columns), lambda j, part_ref: (0, part_ref[0] * steps + j)),
            ],
            out_specs=pl.BlockSpec((tok_rows, columns), lambda j, part_ref: (0, j)),
            scratch_shapes=[pltpu.VMEM((tok_rows, depth), token_heads.dtype)],
        ),
        out_shape=jax.ShapeDtypeStruct((tok_rows, width), dtype),
        name="project_part",
    )(jnp.reshape(part, (1,)), token_heads, w_out)


def to_heads(shard, head_dim, seq_count):
    tok_rows = shard.shape[0]
    by_head = jnp.transpose(shard.reshape(tok_rows, seq_count, head_dim), (1, 0, 2))
    return lax.all_to_all(by_head, "seq", split_axis=0, concat_axis=0, tiled=True)


def local_by_head(shared_qk, values, buckets, counts, w_out):
    tok_rows = shared_qk.shape[0]
    head_count = buckets.shape[1]
    head_dim = shared_qk.shape[1] // head_count
    seq_count = lax.axis_size("seq")
    part_count = lax.axis_size("mp")
    token_count = tok_rows * seq_count
    bucket_count = counts.shape[2]
    head_buckets = lax.all_to_all(buckets.T, "seq", split_axis=0, concat_axis=0, tiled=True)
    head_qk = to_heads(shared_qk, head_dim, seq_count)
    head_qk, values = lax.optimization_barrier((head_qk, values))
    head_values = to_heads(values, head_dim, seq_count)
    weights = head_weights(head_buckets, head_qk.reshape(token_count, head_dim), bucket_count)
    attended = head_attend(weights, head_values.reshape(token_count, head_dim))
    token_heads = lax.all_to_all(
        attended.reshape(seq_count, tok_rows, head_dim), "seq", split_axis=0, concat_axis=0, tiled=True
    )
    part = lax.axis_index("mp")
    theirs = project_part(token_heads, w_out, 1 - part, part_count, jnp.bfloat16)
    arrived = lax.ppermute(theirs, "mp", [(0, 1), (1, 0)])
    ours = project_part(token_heads, w_out, part, part_count, jnp.float32)
    return (ours + arrived.astype(jnp.float32)).astype(jnp.bfloat16)


def local(shared_qk, values, buckets, counts, w_out):
    head_count = buckets.shape[1]
    seq_count = lax.axis_size("seq")
    one_head_each = head_count == seq_count and counts.shape[2] == seq_count and 2 < seq_count <= 128
    if one_head_each and lax.axis_size("mp") == 2 and 2 * shared_qk.shape[0] <= BLOCK:
        return local_by_head(shared_qk, values, buckets, counts, w_out)
    return local_by_bucket(shared_qk, values, buckets, counts, w_out)


def solution(mesh):
    placed = (P("seq", "mp"), P("seq", "mp"), P("seq", "mp"), P(None, "mp", None), P("mp", None))
    return jax.shard_map(
        local, mesh=mesh, in_specs=placed, out_specs=P("seq", "mp"), check_vma=False
    )
```

```python
import functools
import math

import jax
import jax.numpy as jnp
from jax import lax
from jax.experimental import pallas as pl
from jax.experimental.pallas import tpu as pltpu
from jax.sharding import PartitionSpec as P

BLOCK = 256
MASKED = -1e30


SELF_SCORE = -100000.0


def passed_along(shard, axis, by):
    devices = lax.axis_size(axis)
    return lax.ppermute(shard, axis, [(i, (i + by) % devices) for i in range(devices)])


def block_attention(queries, window, window_live):
    head_dim = queries.shape[-1]
    block_rows = queries.shape[-2]
    key_rows = window[..., :head_dim]
    value_rows = window[..., head_dim:]
    scores = jnp.einsum("cqd,ckd->cqk", queries, key_rows, preferred_element_type=jnp.float32) * (
        1.0 / math.sqrt(head_dim)
    )
    query_place = jnp.arange(block_rows)[:, None] + block_rows
    key_place = jnp.arange(2 * block_rows)[None, :]
    itself = query_place == key_place
    scores = jnp.where(itself[None], SELF_SCORE, scores)
    allowed = window_live[:, None, :] | itself[None]
    row_max = jnp.max(jnp.where(allowed, scores, -1e30), axis=-1, keepdims=True)
    exp_terms = jnp.where(allowed, jnp.exp(scores - row_max), 0.0)
    weights = (exp_terms / jnp.sum(exp_terms, axis=-1, keepdims=True)).astype(jnp.bfloat16)
    attended = jnp.einsum("cqk,ckd->cqd", weights, value_rows, preferred_element_type=jnp.float32)
    return attended.astype(jnp.bfloat16)


def owner_layout(received, column, slot_count):
    source_count = column.shape[0]
    head_count = column.shape[1]
    upto_count = jnp.cumsum(column, axis=0)
    before_count = upto_count - column
    bucket_total = upto_count[-1]
    slot_range = jnp.arange(slot_count)
    source_dev = jnp.sum(upto_count[:, :, None] <= slot_range[None, None, :], axis=0)
    source_dev = jnp.minimum(source_dev, source_count - 1)
    source_range = jnp.arange(source_count)
    source_start = jnp.sum(
        jnp.where(source_dev[None] == source_range[:, None, None], before_count[:, :, None], 0),
        axis=0,
    )
    entry_row = jnp.clip(slot_range[None, :] - source_start, 0, received.shape[2] - 1)
    head_range = jnp.arange(head_count)
    layout = received[source_dev, head_range[:, None], entry_row]
    live = slot_range[None, :] < bucket_total[:, None]
    layout = jnp.where(live[..., None], layout, jnp.zeros((), layout.dtype))
    return (layout, live, before_count, bucket_total)


def tail_live(bucket_total, block_rows):
    return bucket_total[:, None] - block_rows + jnp.arange(block_rows)[None, :] >= 0


def last_rows(layout, bucket_total, block_rows):
    rank_index = bucket_total[:, None] - block_rows + jnp.arange(block_rows)[None, :]
    head_range = jnp.arange(layout.shape[0])
    rows = layout[head_range[:, None], jnp.maximum(rank_index, 0)]
    return jnp.where((rank_index >= 0)[..., None], rows, jnp.zeros((), rows.dtype))


def local_by_bucket(shared_qk, values, buckets, counts, w_out):
    tok_rows = shared_qk.shape[0]
    head_count = buckets.shape[1]
    head_dim = shared_qk.shape[1] // head_count
    seq_count = lax.axis_size("seq")
    capacity = 2 * tok_rows // seq_count
    slot_count = seq_count * capacity
    block_rows = BLOCK
    block_count = slot_count // block_rows
    own_index = lax.axis_index("seq")
    prev_index = (own_index + seq_count - 1) % seq_count
    head_range = jnp.arange(head_count)
    bucket_heads = buckets.T
    positions = jnp.arange(tok_rows)
    earlier = positions[None, :] < positions[:, None]
    same_bucket = bucket_heads[:, :, None] == bucket_heads[:, None, :]
    within = jnp.sum(same_bucket & earlier[None], axis=2)
    own_counts = lax.dynamic_index_in_dim(counts, own_index, 0, keepdims=False)
    own_starts = jnp.cumsum(own_counts, axis=1) - own_counts
    bucket_range = jnp.arange(seq_count)
    one_hot = bucket_heads[:, :, None] == bucket_range[None, None, :]
    token_start = jnp.sum(jnp.where(one_hot, own_starts[:, None, :], 0), axis=2)
    sorted_pos = token_start + within
    token_order = jnp.sum(
        jnp.where(sorted_pos[:, :, None] == positions[None, None, :], positions[None, :, None], 0),
        axis=1,
    )
    slot_range = jnp.arange(capacity)
    send_index = own_starts.T[:, :, None] + slot_range[None, None, :]
    filled = slot_range[None, None, :] < own_counts.T[:, :, None]
    token_pick = token_order[head_range[None, :, None], jnp.minimum(send_index, tok_rows - 1)]
    packed = jnp.concatenate(
        [
            shared_qk.reshape(tok_rows, head_count, head_dim),
            values.reshape(tok_rows, head_count, head_dim),
        ],
        axis=2,
    )
    outgoing = packed[token_pick, head_range[None, :, None]]
    outgoing = jnp.where(filled[..., None], outgoing, jnp.zeros((), outgoing.dtype))
    own_column = lax.dynamic_index_in_dim(counts, own_index, 2, keepdims=False)
    prev_column = lax.dynamic_index_in_dim(counts, prev_index, 2, keepdims=False)
    prev_total = jnp.sum(prev_column, axis=0)
    received = lax.all_to_all(outgoing, "seq", split_axis=0, concat_axis=0, tiled=True)
    layout, live, before_count, bucket_total = owner_layout(received, own_column, slot_count)
    tail_rows = last_rows(layout, bucket_total, block_rows)
    prev_rows = passed_along(tail_rows, "seq", 1)
    prev_live = tail_live(prev_total, block_rows)
    keys_all = jnp.concatenate([prev_rows, layout], axis=1)
    live_all = jnp.concatenate([prev_live, live], axis=1)
    window = jnp.concatenate(
        [
            keys_all[:, :slot_count].reshape(head_count, block_count, block_rows, 2 * head_dim),
            keys_all[:, block_rows:].reshape(head_count, block_count, block_rows, 2 * head_dim),
        ],
        axis=2,
    )
    window_live = jnp.concatenate(
        [
            live_all[:, :slot_count].reshape(head_count, block_count, block_rows),
            live_all[:, block_rows:].reshape(head_count, block_count, block_rows),
        ],
        axis=2,
    )
    queries = layout[..., :head_dim].reshape(head_count, block_count, block_rows, head_dim)
    attended = lax.map(
        lambda per_head: block_attention(per_head[0], per_head[1], per_head[2]),
        (queries, window, window_live),
    )
    out_layout = attended.reshape(head_count, slot_count, head_dim)
    back_index = before_count[:, :, None] + slot_range[None, None, :]
    back_filled = slot_range[None, None, :] < own_column[:, :, None]
    back_rows = out_layout[head_range[None, :, None], jnp.minimum(back_index, slot_count - 1)]
    back_rows = jnp.where(back_filled[..., None], back_rows, jnp.zeros((), back_rows.dtype))
    returned = lax.all_to_all(back_rows, "seq", split_axis=0, concat_axis=0, tiled=True)
    token_out = returned[buckets, head_range[None, :], within.T]
    token_out = token_out.reshape(tok_rows, head_count * head_dim)
    partial_sum = jnp.dot(token_out, w_out, preferred_element_type=jnp.float32)
    projected = lax.psum_scatter(partial_sum, "mp", scatter_dimension=1, tiled=True)
    return projected.astype(jnp.bfloat16)


PAD_ROWS = 8


def in_vmem(count):
    return [pl.BlockSpec(memory_space=pltpu.VMEM)] * count


def in_hbm(count):
    return [pl.BlockSpec(memory_space=pltpu.HBM)] * count


def stays_in_hbm(array):
    return pltpu.with_memory_space_constraint(array, pltpu.HBM)


def vmem_params(mebibytes):
    return pltpu.CompilerParams(vmem_limit_bytes=mebibytes * 2**20)


def pack_kernel(bucket_hbm, qk_hbm, value_hbm, out_ref, bucket_ref, sems):
    head_count, rows, head_dim = out_ref.shape
    tok_rows = qk_hbm.shape[0]
    copies = [pltpu.make_async_copy(bucket_hbm, bucket_ref, sems.at[2 * head_count])]
    for head in range(head_count):
        for which, source in enumerate((qk_hbm, value_hbm)):
            copies.append(
                pltpu.make_async_copy(
                    source.at[:, head * head_dim : (head + 1) * head_dim],
                    out_ref.at[head, which * tok_rows : (which + 1) * tok_rows, :],
                    sems.at[2 * head + which],
                )
            )
    for copy in copies:
        copy.start()
    copies[0].wait()
    for head in range(head_count):
        bucket = bucket_ref[head : head + 1, :].astype(jnp.float32)
        out_ref[head, 2 * tok_rows :, :] = jnp.broadcast_to(bucket, (PAD_ROWS, tok_rows)).astype(out_ref.dtype)
    for copy in copies[1:]:
        copy.wait()


def pack_heads(bucket_heads, shared_qk, values):
    head_count, tok_rows = bucket_heads.shape
    head_dim = shared_qk.shape[1] // head_count
    return pl.pallas_call(
        pack_kernel,
        in_specs=in_hbm(3),
        out_specs=in_vmem(1)[0],
        out_shape=pltpu.VMEM((head_count, 2 * tok_rows + PAD_ROWS, head_dim), shared_qk.dtype),
        scratch_shapes=[
            pltpu.VMEM(bucket_heads.shape, bucket_heads.dtype),
            pltpu.SemaphoreType.DMA((2 * head_count + 1,)),
        ],
        compiler_params=vmem_params(8),
        name="pack_heads",
    )(*(stays_in_hbm(array) for array in (bucket_heads, shared_qk, values)))


def attend_kernel(
    in_ref, w_hbm, out_ref, w_ref, query_ref, key_ref, value_ref, *scratch, bucket_count, query_rows
):
    source_count, tok_rows, head_dim = out_ref.shape
    token_count = source_count * tok_rows
    score_refs, term_refs, sem = scratch[:2], scratch[2:4], scratch[4]
    width = w_ref.shape[1]
    theirs = pl.multiple_of((1 - lax.axis_index("mp")) * width, width)
    fetch = pltpu.make_async_copy(w_hbm.at[:, pl.ds(theirs, width)], w_ref, sem)
    fetch.start()
    lane = lax.broadcasted_iota(jnp.int32, (tok_rows, head_dim), 1)
    for source in range(source_count):
        at = slice(source * tok_rows, (source + 1) * tok_rows)
        query_ref[at, :head_dim] = in_ref[source, :tok_rows, :]
        key_ref[at, :head_dim] = in_ref[source, :tok_rows, :]
        value_ref[at, :head_dim] = in_ref[source, tok_rows : 2 * tok_rows, :]
        value_ref[at, head_dim:] = jnp.ones((tok_rows, head_dim), value_ref.dtype)
        row = in_ref[source, 2 * tok_rows :, :].astype(jnp.float32)[:1]
        bucket = jnp.broadcast_to(row, (head_dim, tok_rows)).T.astype(jnp.int32)
        following = jnp.where(bucket == bucket_count - 1, 0, bucket + 1)
        own = lane == bucket
        query_ref[at, head_dim:] = jnp.where(own, 1.0, 0.0).astype(query_ref.dtype)
        key_ref[at, head_dim:] = jnp.where(own | (lane == following), 0.0, MASKED).astype(key_ref.dtype)
    scale = 1.0 / math.sqrt(head_dim)
    strip = 16
    square = (tok_rows, tok_rows)
    itself = lax.broadcasted_iota(jnp.int32, square, 0) == lax.broadcasted_iota(jnp.int32, square, 1)

    def scores_of(block, score_ref):
        score_ref[...] = lax.dot_general(
            query_ref[block * query_rows : (block + 1) * query_rows, :],
            key_ref[...],
            (((1,), (1,)), ((), ())),
            preferred_element_type=jnp.float32,
        )
        for at in range(0, query_rows, tok_rows):
            columns = slice(block * query_rows + at, block * query_rows + at + tok_rows)
            own = score_ref[at : at + tok_rows, columns]
            score_ref[at : at + tok_rows, columns] = jnp.where(itself, SELF_SCORE / scale, own)

    def terms_of(score_ref, term_ref):
        for at in range(0, query_rows, strip):
            scores = score_ref[at : at + strip, :]
            row_max = jnp.max(scores, axis=1, keepdims=True)
            terms = jnp.exp2((scores - row_max) * (scale * math.log2(math.e)))
            term_ref[at : at + strip, :] = terms.astype(term_ref.dtype)

    def attend_of(block, term_ref):
        both = jnp.dot(term_ref[...], value_ref[...], preferred_element_type=jnp.float32)
        attended = (both[:, :head_dim] / both[:, head_dim:]).astype(out_ref.dtype)
        for at in range(0, query_rows, tok_rows):
            out_ref[(block * query_rows + at) // tok_rows] = attended[at : at + tok_rows]

    blocks = token_count // query_rows
    scores_of(0, score_refs[0])
    for block in range(blocks):
        if block + 1 < blocks:
            scores_of(block + 1, score_refs[(block + 1) % 2])
        terms_of(score_refs[block % 2], term_refs[block % 2])
        attend_of(block, term_refs[block % 2])
    fetch.wait()


def attend_head(received, w_out, bucket_count):
    source_count, rows, head_dim = received.shape
    tok_rows = (rows - PAD_ROWS) // 2
    token_count = source_count * tok_rows
    query_rows = 2 * tok_rows
    extended = pltpu.VMEM((token_count, 2 * head_dim), received.dtype)
    scores = pltpu.VMEM((query_rows, token_count), jnp.float32)
    terms = pltpu.VMEM((query_rows, token_count), received.dtype)
    return pl.pallas_call(
        functools.partial(attend_kernel, bucket_count=bucket_count, query_rows=query_rows),
        in_specs=in_vmem(1) + in_hbm(1),
        out_specs=tuple(in_vmem(2)),
        out_shape=(
            pltpu.VMEM((source_count, tok_rows, head_dim), received.dtype),
            pltpu.VMEM((w_out.shape[0], w_out.shape[1] // 2), w_out.dtype),
        ),
        scratch_shapes=[
            *(extended, extended, extended, scores, scores, terms, terms),
            pltpu.SemaphoreType.DMA(()),
        ],
        compiler_params=vmem_params(20),
        name="attend_head",
    )(received, stays_in_hbm(w_out))


def widen(token_ref, wide_ref):
    head_count, tok_rows, head_dim = token_ref.shape
    for head in range(head_count):
        wide_ref[:, head * head_dim : (head + 1) * head_dim] = token_ref[head]


def theirs_kernel(token_ref, w_ref, out_ref, wide_ref, *, chunk):
    widen(token_ref, wide_ref)
    columns = out_ref.shape[1]
    out_ref[...] = jnp.dot(
        wide_ref[...], w_ref[:, chunk * columns : (chunk + 1) * columns], preferred_element_type=jnp.float32
    ).astype(out_ref.dtype)


def project_theirs(token_heads, w_theirs, chunk, chunks):
    head_count, tok_rows, head_dim = token_heads.shape
    depth, features = w_theirs.shape
    return pl.pallas_call(
        functools.partial(theirs_kernel, chunk=chunk),
        in_specs=in_vmem(2),
        out_specs=in_vmem(1)[0],
        out_shape=pltpu.VMEM((tok_rows, features // chunks), token_heads.dtype),
        scratch_shapes=[pltpu.VMEM((tok_rows, depth), token_heads.dtype)],
        compiler_params=vmem_params(16),
        name="project_theirs",
    )(token_heads, w_theirs)


def ours_kernel(token_ref, w_hbm, out_ref, wide_ref, w_ref, sems):
    chunks, depth, columns = w_ref.shape
    start = pl.multiple_of(lax.axis_index("mp") * (chunks * columns), columns)
    copies = [
        pltpu.make_async_copy(w_hbm.at[:, pl.ds(start + chunk * columns, columns)], w_ref.at[chunk], sems.at[chunk])
        for chunk in range(chunks)
    ]
    for copy in copies:
        copy.start()
    widen(token_ref, wide_ref)
    for chunk, copy in enumerate(copies):
        copy.wait()
        out_ref[:, chunk * columns : (chunk + 1) * columns] = jnp.dot(
            wide_ref[...], w_ref[chunk], preferred_element_type=jnp.float32
        )


def project_ours(token_heads, w_out):
    head_count, tok_rows, head_dim = token_heads.shape
    depth, features = w_out.shape
    chunks = 4
    columns = features // (2 * chunks)
    return pl.pallas_call(
        ours_kernel,
        in_specs=in_vmem(1) + in_hbm(1),
        out_specs=in_vmem(1)[0],
        out_shape=pltpu.VMEM((tok_rows, chunks * columns), jnp.float32),
        scratch_shapes=[
            pltpu.VMEM((tok_rows, depth), token_heads.dtype),
            pltpu.VMEM((chunks, depth, columns), w_out.dtype),
            pltpu.SemaphoreType.DMA((chunks,)),
        ],
        compiler_params=vmem_params(20),
        name="project_ours",
    )(token_heads, stays_in_hbm(w_out))


def add_kernel(ours_ref, *refs):
    out_ref = refs[-1]
    columns = refs[0].shape[1]
    for chunk, theirs_ref in enumerate(refs[:-1]):
        at = slice(chunk * columns, (chunk + 1) * columns)
        out_ref[:, at] = (ours_ref[:, at] + theirs_ref[...].astype(jnp.float32)).astype(out_ref.dtype)


def add_parts(ours, theirs, dtype):
    return pl.pallas_call(
        add_kernel,
        in_specs=in_vmem(1 + len(theirs)),
        out_shape=jax.ShapeDtypeStruct(ours.shape, dtype),
        compiler_params=vmem_params(8),
        name="add_parts",
    )(ours, *theirs)


def exchange(blocks):
    return lax.all_to_all(blocks, "seq", split_axis=0, concat_axis=0, tiled=True)


def local_by_head(shared_qk, values, buckets, counts, w_out):
    received = exchange(pack_heads(buckets.T, shared_qk, values))
    attended, w_theirs = attend_head(received, w_out, counts.shape[2])
    token_heads = exchange(attended)
    chunks = 2
    arrived = [
        lax.ppermute(project_theirs(token_heads, w_theirs, chunk, chunks), "mp", [(0, 1), (1, 0)])
        for chunk in range(chunks)
    ]
    ours = project_ours(token_heads, w_out)
    return add_parts(ours, arrived, shared_qk.dtype)


def local(shared_qk, values, buckets, counts, w_out):
    head_count = buckets.shape[1]
    seq_count = lax.axis_size("seq")
    one_head_each = head_count == seq_count and counts.shape[2] == seq_count and 2 < seq_count <= 128
    if one_head_each and lax.axis_size("mp") == 2 and 2 * shared_qk.shape[0] <= BLOCK:
        return local_by_head(shared_qk, values, buckets, counts, w_out)
    return local_by_bucket(shared_qk, values, buckets, counts, w_out)


def solution(mesh):
    placed = (P("seq", "mp"), P("seq", "mp"), P("seq", "mp"), P(None, "mp", None), P("mp", None))
    return jax.shard_map(
        local, mesh=mesh, in_specs=placed, out_specs=P("seq", "mp"), check_vma=False
    )
```

```python
import functools
import math

import jax
import jax.numpy as jnp
from jax import lax
from jax.experimental import pallas as pl
from jax.experimental.pallas import tpu as pltpu
from jax.sharding import PartitionSpec as P

BLOCK = 256
MASKED = -1e30


SELF_SCORE = -100000.0


def passed_along(shard, axis, by):
    devices = lax.axis_size(axis)
    return lax.ppermute(shard, axis, [(i, (i + by) % devices) for i in range(devices)])


def block_attention(queries, window, window_live):
    head_dim = queries.shape[-1]
    block_rows = queries.shape[-2]
    key_rows = window[..., :head_dim]
    value_rows = window[..., head_dim:]
    scores = jnp.einsum("cqd,ckd->cqk", queries, key_rows, preferred_element_type=jnp.float32) * (
        1.0 / math.sqrt(head_dim)
    )
    query_place = jnp.arange(block_rows)[:, None] + block_rows
    key_place = jnp.arange(2 * block_rows)[None, :]
    itself = query_place == key_place
    scores = jnp.where(itself[None], SELF_SCORE, scores)
    allowed = window_live[:, None, :] | itself[None]
    row_max = jnp.max(jnp.where(allowed, scores, -1e30), axis=-1, keepdims=True)
    exp_terms = jnp.where(allowed, jnp.exp(scores - row_max), 0.0)
    weights = (exp_terms / jnp.sum(exp_terms, axis=-1, keepdims=True)).astype(jnp.bfloat16)
    attended = jnp.einsum("cqk,ckd->cqd", weights, value_rows, preferred_element_type=jnp.float32)
    return attended.astype(jnp.bfloat16)


def owner_layout(received, column, slot_count):
    source_count = column.shape[0]
    head_count = column.shape[1]
    upto_count = jnp.cumsum(column, axis=0)
    before_count = upto_count - column
    bucket_total = upto_count[-1]
    slot_range = jnp.arange(slot_count)
    source_dev = jnp.sum(upto_count[:, :, None] <= slot_range[None, None, :], axis=0)
    source_dev = jnp.minimum(source_dev, source_count - 1)
    source_range = jnp.arange(source_count)
    source_start = jnp.sum(
        jnp.where(source_dev[None] == source_range[:, None, None], before_count[:, :, None], 0),
        axis=0,
    )
    entry_row = jnp.clip(slot_range[None, :] - source_start, 0, received.shape[2] - 1)
    head_range = jnp.arange(head_count)
    layout = received[source_dev, head_range[:, None], entry_row]
    live = slot_range[None, :] < bucket_total[:, None]
    layout = jnp.where(live[..., None], layout, jnp.zeros((), layout.dtype))
    return (layout, live, before_count, bucket_total)


def tail_live(bucket_total, block_rows):
    return bucket_total[:, None] - block_rows + jnp.arange(block_rows)[None, :] >= 0


def last_rows(layout, bucket_total, block_rows):
    rank_index = bucket_total[:, None] - block_rows + jnp.arange(block_rows)[None, :]
    head_range = jnp.arange(layout.shape[0])
    rows = layout[head_range[:, None], jnp.maximum(rank_index, 0)]
    return jnp.where((rank_index >= 0)[..., None], rows, jnp.zeros((), rows.dtype))


def local_by_bucket(shared_qk, values, buckets, counts, w_out):
    tok_rows = shared_qk.shape[0]
    head_count = buckets.shape[1]
    head_dim = shared_qk.shape[1] // head_count
    seq_count = lax.axis_size("seq")
    capacity = 2 * tok_rows // seq_count
    slot_count = seq_count * capacity
    block_rows = BLOCK
    block_count = slot_count // block_rows
    own_index = lax.axis_index("seq")
    prev_index = (own_index + seq_count - 1) % seq_count
    head_range = jnp.arange(head_count)
    bucket_heads = buckets.T
    positions = jnp.arange(tok_rows)
    earlier = positions[None, :] < positions[:, None]
    same_bucket = bucket_heads[:, :, None] == bucket_heads[:, None, :]
    within = jnp.sum(same_bucket & earlier[None], axis=2)
    own_counts = lax.dynamic_index_in_dim(counts, own_index, 0, keepdims=False)
    own_starts = jnp.cumsum(own_counts, axis=1) - own_counts
    bucket_range = jnp.arange(seq_count)
    one_hot = bucket_heads[:, :, None] == bucket_range[None, None, :]
    token_start = jnp.sum(jnp.where(one_hot, own_starts[:, None, :], 0), axis=2)
    sorted_pos = token_start + within
    token_order = jnp.sum(
        jnp.where(sorted_pos[:, :, None] == positions[None, None, :], positions[None, :, None], 0),
        axis=1,
    )
    slot_range = jnp.arange(capacity)
    send_index = own_starts.T[:, :, None] + slot_range[None, None, :]
    filled = slot_range[None, None, :] < own_counts.T[:, :, None]
    token_pick = token_order[head_range[None, :, None], jnp.minimum(send_index, tok_rows - 1)]
    packed = jnp.concatenate(
        [
            shared_qk.reshape(tok_rows, head_count, head_dim),
            values.reshape(tok_rows, head_count, head_dim),
        ],
        axis=2,
    )
    outgoing = packed[token_pick, head_range[None, :, None]]
    outgoing = jnp.where(filled[..., None], outgoing, jnp.zeros((), outgoing.dtype))
    own_column = lax.dynamic_index_in_dim(counts, own_index, 2, keepdims=False)
    prev_column = lax.dynamic_index_in_dim(counts, prev_index, 2, keepdims=False)
    prev_total = jnp.sum(prev_column, axis=0)
    received = lax.all_to_all(outgoing, "seq", split_axis=0, concat_axis=0, tiled=True)
    layout, live, before_count, bucket_total = owner_layout(received, own_column, slot_count)
    tail_rows = last_rows(layout, bucket_total, block_rows)
    prev_rows = passed_along(tail_rows, "seq", 1)
    prev_live = tail_live(prev_total, block_rows)
    keys_all = jnp.concatenate([prev_rows, layout], axis=1)
    live_all = jnp.concatenate([prev_live, live], axis=1)
    window = jnp.concatenate(
        [
            keys_all[:, :slot_count].reshape(head_count, block_count, block_rows, 2 * head_dim),
            keys_all[:, block_rows:].reshape(head_count, block_count, block_rows, 2 * head_dim),
        ],
        axis=2,
    )
    window_live = jnp.concatenate(
        [
            live_all[:, :slot_count].reshape(head_count, block_count, block_rows),
            live_all[:, block_rows:].reshape(head_count, block_count, block_rows),
        ],
        axis=2,
    )
    queries = layout[..., :head_dim].reshape(head_count, block_count, block_rows, head_dim)
    attended = lax.map(
        lambda per_head: block_attention(per_head[0], per_head[1], per_head[2]),
        (queries, window, window_live),
    )
    out_layout = attended.reshape(head_count, slot_count, head_dim)
    back_index = before_count[:, :, None] + slot_range[None, None, :]
    back_filled = slot_range[None, None, :] < own_column[:, :, None]
    back_rows = out_layout[head_range[None, :, None], jnp.minimum(back_index, slot_count - 1)]
    back_rows = jnp.where(back_filled[..., None], back_rows, jnp.zeros((), back_rows.dtype))
    returned = lax.all_to_all(back_rows, "seq", split_axis=0, concat_axis=0, tiled=True)
    token_out = returned[buckets, head_range[None, :], within.T]
    token_out = token_out.reshape(tok_rows, head_count * head_dim)
    partial_sum = jnp.dot(token_out, w_out, preferred_element_type=jnp.float32)
    projected = lax.psum_scatter(partial_sum, "mp", scatter_dimension=1, tiled=True)
    return projected.astype(jnp.bfloat16)


PAD_ROWS = 8


def in_vmem(count):
    return [pl.BlockSpec(memory_space=pltpu.VMEM)] * count


def in_hbm(count):
    return [pl.BlockSpec(memory_space=pltpu.HBM)] * count


def stays_in_hbm(array):
    return pltpu.with_memory_space_constraint(array, pltpu.HBM)


def vmem_params(mebibytes):
    return pltpu.CompilerParams(vmem_limit_bytes=mebibytes * 2**20)


def shifts(count):
    stride = math.isqrt(count)
    return sorted(range(1, count), key=lambda shift: (shift % stride, shift))


def block_copies(bucket_hbm, qk_hbm, value_hbm, head, qk_ref, value_ref, sems):
    head_dim = qk_ref.shape[1]
    columns = pl.ds(pl.multiple_of(head * head_dim, head_dim), head_dim)
    return [
        pltpu.make_async_copy(qk_hbm.at[:, columns], qk_ref, sems.at[0]),
        pltpu.make_async_copy(value_hbm.at[:, columns], value_ref, sems.at[1]),
    ]


def pack_kernel(bucket_hbm, qk_hbm, value_hbm, *refs):
    outs, (bucket_ref, bucket_sem, sems) = refs[:-3], refs[-3:]
    head_count = bucket_ref.shape[0]
    tok_rows = qk_hbm.shape[0]
    own = lax.axis_index("seq")
    heads = [(own + shift) % head_count for shift in shifts(head_count)]
    fetch_buckets = pltpu.make_async_copy(bucket_hbm, bucket_ref, bucket_sem)
    fetch_buckets.start()
    copies = []
    for at, (head, out) in enumerate(zip(heads, outs)):
        qk_ref, value_ref = out.at[:tok_rows, :], out.at[tok_rows : 2 * tok_rows, :]
        copies += block_copies(bucket_hbm, qk_hbm, value_hbm, head, qk_ref, value_ref, sems.at[at])
    for copy in copies:
        copy.start()
    fetch_buckets.wait()
    for head, out in zip(heads, outs):
        bucket = bucket_ref[pl.ds(head, 1), :].astype(jnp.float32)
        out[2 * tok_rows :, :] = jnp.broadcast_to(bucket, (PAD_ROWS, tok_rows)).astype(out.dtype)
    for copy in copies:
        copy.wait()


def pack_blocks(bucket_heads, shared_qk, values):
    head_count, tok_rows = bucket_heads.shape
    head_dim = shared_qk.shape[1] // head_count
    block = pltpu.VMEM((2 * tok_rows + PAD_ROWS, head_dim), shared_qk.dtype)
    return pl.pallas_call(
        pack_kernel,
        in_specs=in_hbm(3),
        out_specs=in_vmem(head_count - 1),
        out_shape=[block] * (head_count - 1),
        scratch_shapes=[
            pltpu.VMEM(bucket_heads.shape, bucket_heads.dtype),
            pltpu.SemaphoreType.DMA(()),
            pltpu.SemaphoreType.DMA((head_count - 1, 2)),
        ],
        compiler_params=vmem_params(8),
        name="pack_blocks",
    )(*(stays_in_hbm(array) for array in (bucket_heads, shared_qk, values)))


def attend_kernel(bucket_hbm, qk_hbm, value_hbm, w_hbm, *refs, bucket_count, query_rows):
    source_count = bucket_hbm.shape[0]
    block_refs, (out_ref, w_ref, query_ref, key_ref, value_ref) = refs[: source_count - 1], refs[source_count - 1 : source_count + 4]
    score_refs, term_refs = refs[source_count + 4 : source_count + 6], refs[source_count + 6 : source_count + 8]
    bucket_ref, sems = refs[source_count + 8 :]
    _, tok_rows, head_dim = out_ref.shape
    token_count = source_count * tok_rows
    own = lax.axis_index("seq")
    owners = [own] + [(own + source_count - shift) % source_count for shift in shifts(source_count)]
    first = slice(0, tok_rows)
    own_copies = block_copies(
        bucket_hbm, qk_hbm, value_hbm, own, key_ref.at[first, :head_dim], value_ref.at[first, :head_dim], sems
    )
    own_copies.append(pltpu.make_async_copy(bucket_hbm, bucket_ref, sems.at[2]))
    for copy in own_copies:
        copy.start()
    width = w_ref.shape[1]
    theirs = pl.multiple_of((1 - lax.axis_index("mp")) * width, width)
    fetch = pltpu.make_async_copy(w_hbm.at[:, pl.ds(theirs, width)], w_ref, sems.at[3])
    fetch.start()
    lane = lax.broadcasted_iota(jnp.int32, (tok_rows, head_dim), 1)
    for source in (*range(1, source_count), 0):
        at = slice(source * tok_rows, (source + 1) * tok_rows)
        if source:
            block_ref = block_refs[source - 1]
            query_ref[at, :head_dim] = block_ref[:tok_rows, :]
            key_ref[at, :head_dim] = block_ref[:tok_rows, :]
            value_ref[at, :head_dim] = block_ref[tok_rows : 2 * tok_rows, :]
            row = block_ref[2 * tok_rows :, :].astype(jnp.float32)[:1]
        else:
            for copy in own_copies:
                copy.wait()
            query_ref[at, :head_dim] = key_ref[at, :head_dim]
            row = bucket_ref[pl.ds(own, 1), :].astype(jnp.float32)
        value_ref[at, head_dim:] = jnp.ones((tok_rows, head_dim), value_ref.dtype)
        bucket = jnp.broadcast_to(row, (head_dim, tok_rows)).T.astype(jnp.int32)
        following = jnp.where(bucket == bucket_count - 1, 0, bucket + 1)
        same = lane == bucket
        query_ref[at, head_dim:] = jnp.where(same, 1.0, 0.0).astype(query_ref.dtype)
        key_ref[at, head_dim:] = jnp.where(same | (lane == following), 0.0, MASKED).astype(key_ref.dtype)
    scale = 1.0 / math.sqrt(head_dim)
    strip = 16
    square = (tok_rows, tok_rows)
    itself = lax.broadcasted_iota(jnp.int32, square, 0) == lax.broadcasted_iota(jnp.int32, square, 1)

    def scores_of(block, score_ref):
        score_ref[...] = lax.dot_general(
            query_ref[block * query_rows : (block + 1) * query_rows, :],
            key_ref[...],
            (((1,), (1,)), ((), ())),
            preferred_element_type=jnp.float32,
        )
        for at in range(0, query_rows, tok_rows):
            columns = slice(block * query_rows + at, block * query_rows + at + tok_rows)
            diagonal = score_ref[at : at + tok_rows, columns]
            score_ref[at : at + tok_rows, columns] = jnp.where(itself, SELF_SCORE / scale, diagonal)

    def terms_of(score_ref, term_ref):
        for at in range(0, query_rows, strip):
            scores = score_ref[at : at + strip, :]
            row_max = jnp.max(scores, axis=1, keepdims=True)
            terms = jnp.exp2((scores - row_max) * (scale * math.log2(math.e)))
            term_ref[at : at + strip, :] = terms.astype(term_ref.dtype)

    def attend_of(block, term_ref):
        both = jnp.dot(term_ref[...], value_ref[...], preferred_element_type=jnp.float32)
        attended = (both[:, :head_dim] / both[:, head_dim:]).astype(out_ref.dtype)
        for at in range(0, query_rows, tok_rows):
            out_ref[owners[(block * query_rows + at) // tok_rows]] = attended[at : at + tok_rows]

    blocks = token_count // query_rows
    scores_of(0, score_refs[0])
    for block in range(blocks):
        if block + 1 < blocks:
            scores_of(block + 1, score_refs[(block + 1) % 2])
        terms_of(score_refs[block % 2], term_refs[block % 2])
        attend_of(block, term_refs[block % 2])
    fetch.wait()


def attend_head(bucket_heads, shared_qk, values, w_out, blocks, bucket_count):
    source_count, tok_rows = bucket_heads.shape
    head_dim = shared_qk.shape[1] // source_count
    token_count = source_count * tok_rows
    query_rows = 2 * tok_rows
    extended = pltpu.VMEM((token_count, 2 * head_dim), shared_qk.dtype)
    scores = pltpu.VMEM((query_rows, token_count), jnp.float32)
    terms = pltpu.VMEM((query_rows, token_count), shared_qk.dtype)
    return pl.pallas_call(
        functools.partial(attend_kernel, bucket_count=bucket_count, query_rows=query_rows),
        in_specs=in_hbm(4) + in_vmem(len(blocks)),
        out_specs=tuple(in_vmem(2)),
        out_shape=(
            pltpu.VMEM((source_count, tok_rows, head_dim), shared_qk.dtype),
            pltpu.VMEM((w_out.shape[0], w_out.shape[1] // 2), w_out.dtype),
        ),
        scratch_shapes=[
            *(extended, extended, extended, scores, scores, terms, terms),
            pltpu.VMEM(bucket_heads.shape, bucket_heads.dtype),
            pltpu.SemaphoreType.DMA((4,)),
        ],
        compiler_params=vmem_params(20),
        name="attend_head",
    )(*(stays_in_hbm(array) for array in (bucket_heads, shared_qk, values, w_out)), *blocks)


def widen(token_ref, wide_ref):
    head_count, tok_rows, head_dim = token_ref.shape
    for head in range(head_count):
        wide_ref[:, head * head_dim : (head + 1) * head_dim] = token_ref[head]


def theirs_kernel(token_ref, w_ref, out_ref, wide_ref, *, chunk):
    widen(token_ref, wide_ref)
    columns = out_ref.shape[1]
    out_ref[...] = jnp.dot(
        wide_ref[...], w_ref[:, chunk * columns : (chunk + 1) * columns], preferred_element_type=jnp.float32
    ).astype(out_ref.dtype)


def project_theirs(token_heads, w_theirs, chunk, chunks):
    head_count, tok_rows, head_dim = token_heads.shape
    depth, features = w_theirs.shape
    return pl.pallas_call(
        functools.partial(theirs_kernel, chunk=chunk),
        in_specs=in_vmem(2),
        out_specs=in_vmem(1)[0],
        out_shape=pltpu.VMEM((tok_rows, features // chunks), token_heads.dtype),
        scratch_shapes=[pltpu.VMEM((tok_rows, depth), token_heads.dtype)],
        compiler_params=vmem_params(16),
        name="project_theirs",
    )(token_heads, w_theirs)


def ours_kernel(token_ref, w_hbm, out_ref, wide_ref, w_ref, sems):
    chunks, depth, columns = w_ref.shape
    start = pl.multiple_of(lax.axis_index("mp") * (chunks * columns), columns)
    copies = [
        pltpu.make_async_copy(w_hbm.at[:, pl.ds(start + chunk * columns, columns)], w_ref.at[chunk], sems.at[chunk])
        for chunk in range(chunks)
    ]
    for copy in copies:
        copy.start()
    widen(token_ref, wide_ref)
    for chunk, copy in enumerate(copies):
        copy.wait()
        out_ref[:, chunk * columns : (chunk + 1) * columns] = jnp.dot(
            wide_ref[...], w_ref[chunk], preferred_element_type=jnp.float32
        )


def project_ours(token_heads, w_out):
    head_count, tok_rows, head_dim = token_heads.shape
    depth, features = w_out.shape
    chunks = 4
    columns = features // (2 * chunks)
    return pl.pallas_call(
        ours_kernel,
        in_specs=in_vmem(1) + in_hbm(1),
        out_specs=in_vmem(1)[0],
        out_shape=pltpu.VMEM((tok_rows, chunks * columns), jnp.float32),
        scratch_shapes=[
            pltpu.VMEM((tok_rows, depth), token_heads.dtype),
            pltpu.VMEM((chunks, depth, columns), w_out.dtype),
            pltpu.SemaphoreType.DMA((chunks,)),
        ],
        compiler_params=vmem_params(20),
        name="project_ours",
    )(token_heads, stays_in_hbm(w_out))


def add_kernel(ours_ref, *refs):
    out_ref = refs[-1]
    columns = refs[0].shape[1]
    for chunk, theirs_ref in enumerate(refs[:-1]):
        at = slice(chunk * columns, (chunk + 1) * columns)
        out_ref[:, at] = (ours_ref[:, at] + theirs_ref[...].astype(jnp.float32)).astype(out_ref.dtype)


def add_parts(ours, theirs, dtype):
    return pl.pallas_call(
        add_kernel,
        in_specs=in_vmem(1 + len(theirs)),
        out_shape=jax.ShapeDtypeStruct(ours.shape, dtype),
        compiler_params=vmem_params(8),
        name="add_parts",
    )(ours, *theirs)


def exchange(blocks):
    return lax.all_to_all(blocks, "seq", split_axis=0, concat_axis=0, tiled=True)


def local_by_head(shared_qk, values, buckets, counts, w_out):
    bucket_heads = buckets.T
    seq_count = lax.axis_size("seq")
    received = [
        passed_along(block, "seq", shift)
        for shift, block in zip(shifts(seq_count), pack_blocks(bucket_heads, shared_qk, values))
    ]
    attended, w_theirs = attend_head(bucket_heads, shared_qk, values, w_out, received, counts.shape[2])
    token_heads = exchange(attended)
    chunks = 2
    arrived = [
        lax.ppermute(project_theirs(token_heads, w_theirs, chunk, chunks), "mp", [(0, 1), (1, 0)])
        for chunk in range(chunks)
    ]
    ours = project_ours(token_heads, w_out)
    return add_parts(ours, arrived, shared_qk.dtype)


def local(shared_qk, values, buckets, counts, w_out):
    head_count = buckets.shape[1]
    seq_count = lax.axis_size("seq")
    one_head_each = head_count == seq_count and counts.shape[2] == seq_count and 2 < seq_count <= 128
    if one_head_each and lax.axis_size("mp") == 2 and 2 * shared_qk.shape[0] <= BLOCK:
        return local_by_head(shared_qk, values, buckets, counts, w_out)
    return local_by_bucket(shared_qk, values, buckets, counts, w_out)


def solution(mesh):
    placed = (P("seq", "mp"), P("seq", "mp"), P("seq", "mp"), P(None, "mp", None), P("mp", None))
    return jax.shard_map(
        local, mesh=mesh, in_specs=placed, out_specs=P("seq", "mp"), check_vma=False
    )
```

```python
import functools
import math

import jax
import jax.numpy as jnp
from jax import lax
from jax.experimental import pallas as pl
from jax.experimental.pallas import tpu as pltpu
from jax.sharding import PartitionSpec as P

BLOCK = 256
MASKED = -1e30


SELF_SCORE = -100000.0


def passed_along(shard, axis, by):
    devices = lax.axis_size(axis)
    return lax.ppermute(shard, axis, [(i, (i + by) % devices) for i in range(devices)])


def block_attention(queries, window, window_live):
    head_dim = queries.shape[-1]
    block_rows = queries.shape[-2]
    key_rows = window[..., :head_dim]
    value_rows = window[..., head_dim:]
    scores = jnp.einsum("cqd,ckd->cqk", queries, key_rows, preferred_element_type=jnp.float32) * (
        1.0 / math.sqrt(head_dim)
    )
    query_place = jnp.arange(block_rows)[:, None] + block_rows
    key_place = jnp.arange(2 * block_rows)[None, :]
    itself = query_place == key_place
    scores = jnp.where(itself[None], SELF_SCORE, scores)
    allowed = window_live[:, None, :] | itself[None]
    row_max = jnp.max(jnp.where(allowed, scores, -1e30), axis=-1, keepdims=True)
    exp_terms = jnp.where(allowed, jnp.exp(scores - row_max), 0.0)
    weights = (exp_terms / jnp.sum(exp_terms, axis=-1, keepdims=True)).astype(jnp.bfloat16)
    attended = jnp.einsum("cqk,ckd->cqd", weights, value_rows, preferred_element_type=jnp.float32)
    return attended.astype(jnp.bfloat16)


def owner_layout(received, column, slot_count):
    source_count = column.shape[0]
    head_count = column.shape[1]
    upto_count = jnp.cumsum(column, axis=0)
    before_count = upto_count - column
    bucket_total = upto_count[-1]
    slot_range = jnp.arange(slot_count)
    source_dev = jnp.sum(upto_count[:, :, None] <= slot_range[None, None, :], axis=0)
    source_dev = jnp.minimum(source_dev, source_count - 1)
    source_range = jnp.arange(source_count)
    source_start = jnp.sum(
        jnp.where(source_dev[None] == source_range[:, None, None], before_count[:, :, None], 0),
        axis=0,
    )
    entry_row = jnp.clip(slot_range[None, :] - source_start, 0, received.shape[2] - 1)
    head_range = jnp.arange(head_count)
    layout = received[source_dev, head_range[:, None], entry_row]
    live = slot_range[None, :] < bucket_total[:, None]
    layout = jnp.where(live[..., None], layout, jnp.zeros((), layout.dtype))
    return (layout, live, before_count, bucket_total)


def tail_live(bucket_total, block_rows):
    return bucket_total[:, None] - block_rows + jnp.arange(block_rows)[None, :] >= 0


def last_rows(layout, bucket_total, block_rows):
    rank_index = bucket_total[:, None] - block_rows + jnp.arange(block_rows)[None, :]
    head_range = jnp.arange(layout.shape[0])
    rows = layout[head_range[:, None], jnp.maximum(rank_index, 0)]
    return jnp.where((rank_index >= 0)[..., None], rows, jnp.zeros((), rows.dtype))


def local_by_bucket(shared_qk, values, buckets, counts, w_out):
    tok_rows = shared_qk.shape[0]
    head_count = buckets.shape[1]
    head_dim = shared_qk.shape[1] // head_count
    seq_count = lax.axis_size("seq")
    capacity = 2 * tok_rows // seq_count
    slot_count = seq_count * capacity
    block_rows = BLOCK
    block_count = slot_count // block_rows
    own_index = lax.axis_index("seq")
    prev_index = (own_index + seq_count - 1) % seq_count
    head_range = jnp.arange(head_count)
    bucket_heads = buckets.T
    positions = jnp.arange(tok_rows)
    earlier = positions[None, :] < positions[:, None]
    same_bucket = bucket_heads[:, :, None] == bucket_heads[:, None, :]
    within = jnp.sum(same_bucket & earlier[None], axis=2)
    own_counts = lax.dynamic_index_in_dim(counts, own_index, 0, keepdims=False)
    own_starts = jnp.cumsum(own_counts, axis=1) - own_counts
    bucket_range = jnp.arange(seq_count)
    one_hot = bucket_heads[:, :, None] == bucket_range[None, None, :]
    token_start = jnp.sum(jnp.where(one_hot, own_starts[:, None, :], 0), axis=2)
    sorted_pos = token_start + within
    token_order = jnp.sum(
        jnp.where(sorted_pos[:, :, None] == positions[None, None, :], positions[None, :, None], 0),
        axis=1,
    )
    slot_range = jnp.arange(capacity)
    send_index = own_starts.T[:, :, None] + slot_range[None, None, :]
    filled = slot_range[None, None, :] < own_counts.T[:, :, None]
    token_pick = token_order[head_range[None, :, None], jnp.minimum(send_index, tok_rows - 1)]
    packed = jnp.concatenate(
        [
            shared_qk.reshape(tok_rows, head_count, head_dim),
            values.reshape(tok_rows, head_count, head_dim),
        ],
        axis=2,
    )
    outgoing = packed[token_pick, head_range[None, :, None]]
    outgoing = jnp.where(filled[..., None], outgoing, jnp.zeros((), outgoing.dtype))
    own_column = lax.dynamic_index_in_dim(counts, own_index, 2, keepdims=False)
    prev_column = lax.dynamic_index_in_dim(counts, prev_index, 2, keepdims=False)
    prev_total = jnp.sum(prev_column, axis=0)
    received = lax.all_to_all(outgoing, "seq", split_axis=0, concat_axis=0, tiled=True)
    layout, live, before_count, bucket_total = owner_layout(received, own_column, slot_count)
    tail_rows = last_rows(layout, bucket_total, block_rows)
    prev_rows = passed_along(tail_rows, "seq", 1)
    prev_live = tail_live(prev_total, block_rows)
    keys_all = jnp.concatenate([prev_rows, layout], axis=1)
    live_all = jnp.concatenate([prev_live, live], axis=1)
    window = jnp.concatenate(
        [
            keys_all[:, :slot_count].reshape(head_count, block_count, block_rows, 2 * head_dim),
            keys_all[:, block_rows:].reshape(head_count, block_count, block_rows, 2 * head_dim),
        ],
        axis=2,
    )
    window_live = jnp.concatenate(
        [
            live_all[:, :slot_count].reshape(head_count, block_count, block_rows),
            live_all[:, block_rows:].reshape(head_count, block_count, block_rows),
        ],
        axis=2,
    )
    queries = layout[..., :head_dim].reshape(head_count, block_count, block_rows, head_dim)
    attended = lax.map(
        lambda per_head: block_attention(per_head[0], per_head[1], per_head[2]),
        (queries, window, window_live),
    )
    out_layout = attended.reshape(head_count, slot_count, head_dim)
    back_index = before_count[:, :, None] + slot_range[None, None, :]
    back_filled = slot_range[None, None, :] < own_column[:, :, None]
    back_rows = out_layout[head_range[None, :, None], jnp.minimum(back_index, slot_count - 1)]
    back_rows = jnp.where(back_filled[..., None], back_rows, jnp.zeros((), back_rows.dtype))
    returned = lax.all_to_all(back_rows, "seq", split_axis=0, concat_axis=0, tiled=True)
    token_out = returned[buckets, head_range[None, :], within.T]
    token_out = token_out.reshape(tok_rows, head_count * head_dim)
    partial_sum = jnp.dot(token_out, w_out, preferred_element_type=jnp.float32)
    projected = lax.psum_scatter(partial_sum, "mp", scatter_dimension=1, tiled=True)
    return projected.astype(jnp.bfloat16)


PAD_ROWS = 8


def in_vmem(count):
    return [pl.BlockSpec(memory_space=pltpu.VMEM)] * count


def in_hbm(count):
    return [pl.BlockSpec(memory_space=pltpu.HBM)] * count


def stays_in_hbm(array):
    return pltpu.with_memory_space_constraint(array, pltpu.HBM)


def vmem_params(mebibytes):
    return pltpu.CompilerParams(vmem_limit_bytes=mebibytes * 2**20)


def moves(count):
    every = [(step, flip) for step in range(count // 2) for flip in range(2)]
    return sorted(every[1:], key=lambda move: (move[0] % 2, move[1], move[0]))


def moved(index, step, flip, count):
    return (index // 2 + step) % (count // 2) * 2 + (index % 2 + flip) % 2


def sent(block, step, flip):
    count = lax.axis_size("seq")
    return lax.ppermute(block, "seq", [(i, moved(i, step, flip, count)) for i in range(count)])


def block_copies(bucket_hbm, qk_hbm, value_hbm, head, qk_ref, value_ref, sems):
    head_dim = qk_ref.shape[1]
    columns = pl.ds(pl.multiple_of(head * head_dim, head_dim), head_dim)
    return [
        pltpu.make_async_copy(qk_hbm.at[:, columns], qk_ref, sems.at[0]),
        pltpu.make_async_copy(value_hbm.at[:, columns], value_ref, sems.at[1]),
    ]


def pack_kernel(bucket_hbm, qk_hbm, value_hbm, *refs):
    outs, (bucket_ref, bucket_sem, sems) = refs[:-3], refs[-3:]
    head_count = bucket_ref.shape[0]
    tok_rows = qk_hbm.shape[0]
    own = lax.axis_index("seq")
    heads = [moved(own, step, flip, head_count) for step, flip in moves(head_count)]
    fetch_buckets = pltpu.make_async_copy(bucket_hbm, bucket_ref, bucket_sem)
    fetch_buckets.start()
    copies = []
    for at, (head, out) in enumerate(zip(heads, outs)):
        qk_ref, value_ref = out.at[:tok_rows, :], out.at[tok_rows : 2 * tok_rows, :]
        copies += block_copies(bucket_hbm, qk_hbm, value_hbm, head, qk_ref, value_ref, sems.at[at])
    for copy in copies:
        copy.start()
    fetch_buckets.wait()
    for head, out in zip(heads, outs):
        bucket = bucket_ref[pl.ds(head, 1), :].astype(jnp.float32)
        out[2 * tok_rows :, :] = jnp.broadcast_to(bucket, (PAD_ROWS, tok_rows)).astype(out.dtype)
    for copy in copies:
        copy.wait()


def pack_blocks(bucket_heads, shared_qk, values):
    head_count, tok_rows = bucket_heads.shape
    head_dim = shared_qk.shape[1] // head_count
    block = pltpu.VMEM((2 * tok_rows + PAD_ROWS, head_dim), shared_qk.dtype)
    return pl.pallas_call(
        pack_kernel,
        in_specs=in_hbm(3),
        out_specs=in_vmem(head_count - 1),
        out_shape=[block] * (head_count - 1),
        scratch_shapes=[
            pltpu.VMEM(bucket_heads.shape, bucket_heads.dtype),
            pltpu.SemaphoreType.DMA(()),
            pltpu.SemaphoreType.DMA((head_count - 1, 2)),
        ],
        compiler_params=vmem_params(8),
        name="pack_blocks",
    )(*(stays_in_hbm(array) for array in (bucket_heads, shared_qk, values)))


def attend_kernel(bucket_hbm, qk_hbm, value_hbm, w_hbm, *refs, bucket_count, query_rows):
    source_count = bucket_hbm.shape[0]
    pair_count = source_count // 2
    block_refs, refs = refs[: source_count - 1], refs[source_count - 1 :]
    out_refs, refs = refs[:pair_count], refs[pair_count:]
    w_ref, query_ref, key_ref, value_ref = refs[:4]
    score_refs, term_refs = refs[4:6], refs[6:8]
    bucket_ref, sems = refs[8:]
    _, tok_rows, head_dim = out_refs[0].shape
    token_count = source_count * tok_rows
    own = lax.axis_index("seq")
    owners = [(-step % pair_count, (own + flip) % 2) for step, flip in (*moves(source_count), (0, 0))]
    last = slice(token_count - tok_rows, token_count)
    own_copies = block_copies(
        bucket_hbm, qk_hbm, value_hbm, own, key_ref.at[last, :head_dim], value_ref.at[last, :head_dim], sems
    )
    own_copies.append(pltpu.make_async_copy(bucket_hbm, bucket_ref, sems.at[2]))
    for copy in own_copies:
        copy.start()
    width = w_ref.shape[1]
    theirs = pl.multiple_of((1 - lax.axis_index("mp")) * width, width)
    fetch = pltpu.make_async_copy(w_hbm.at[:, pl.ds(theirs, width)], w_ref, sems.at[3])
    fetch.start()
    lane = lax.broadcasted_iota(jnp.int32, (tok_rows, head_dim), 1)

    def prepare(source):
        at = slice(source * tok_rows, (source + 1) * tok_rows)
        if source < source_count - 1:
            block_ref = block_refs[source]
            query_ref[at, :head_dim] = block_ref[:tok_rows, :]
            key_ref[at, :head_dim] = block_ref[:tok_rows, :]
            value_ref[at, :head_dim] = block_ref[tok_rows : 2 * tok_rows, :]
            row = block_ref[2 * tok_rows :, :].astype(jnp.float32)[:1]
        else:
            for copy in own_copies:
                copy.wait()
            query_ref[at, :head_dim] = key_ref[at, :head_dim]
            row = bucket_ref[pl.ds(own, 1), :].astype(jnp.float32)
        value_ref[at, head_dim:] = jnp.ones((tok_rows, head_dim), value_ref.dtype)
        bucket = jnp.broadcast_to(row, (head_dim, tok_rows)).T.astype(jnp.int32)
        following = jnp.where(bucket == bucket_count - 1, 0, bucket + 1)
        same = lane == bucket
        query_ref[at, head_dim:] = jnp.where(same, 1.0, 0.0).astype(query_ref.dtype)
        key_ref[at, head_dim:] = jnp.where(same | (lane == following), 0.0, MASKED).astype(key_ref.dtype)

    scale = 1.0 / math.sqrt(head_dim)
    strip = 16
    square = (tok_rows, tok_rows)
    itself = lax.broadcasted_iota(jnp.int32, square, 0) == lax.broadcasted_iota(jnp.int32, square, 1)

    def scores_of(block, score_ref, keys):
        score_ref[:, keys] = lax.dot_general(
            query_ref[block * query_rows : (block + 1) * query_rows, :],
            key_ref[keys, :],
            (((1,), (1,)), ((), ())),
            preferred_element_type=jnp.float32,
        )

    def replace_diagonal(block, score_ref):
        for at in range(0, query_rows, tok_rows):
            columns = slice(block * query_rows + at, block * query_rows + at + tok_rows)
            diagonal = score_ref[at : at + tok_rows, columns]
            score_ref[at : at + tok_rows, columns] = jnp.where(itself, SELF_SCORE / scale, diagonal)

    def terms_of(score_ref, term_ref):
        for at in range(0, query_rows, strip):
            scores = score_ref[at : at + strip, :]
            row_max = jnp.max(scores, axis=1, keepdims=True)
            terms = jnp.exp2((scores - row_max) * (scale * math.log2(math.e)))
            term_ref[at : at + strip, :] = terms.astype(term_ref.dtype)

    def attend_of(block, term_ref):
        both = jnp.dot(term_ref[...], value_ref[...], preferred_element_type=jnp.float32)
        attended = (both[:, :head_dim] / both[:, head_dim:]).astype(out_refs[0].dtype)
        for at in range(0, query_rows, tok_rows):
            step, which = owners[(block * query_rows + at) // tok_rows]
            out_refs[step][which] = attended[at : at + tok_rows]

    blocks = token_count // query_rows
    for block in range(blocks):
        keys = slice(block * query_rows, (block + 1) * query_rows)
        for source in range(keys.start // tok_rows, keys.stop // tok_rows):
            prepare(source)
        scores_of(0, score_refs[0], keys)
    replace_diagonal(0, score_refs[0])
    for block in range(blocks):
        if block + 1 < blocks:
            scores_of(block + 1, score_refs[(block + 1) % 2], slice(0, token_count))
            replace_diagonal(block + 1, score_refs[(block + 1) % 2])
        terms_of(score_refs[block % 2], term_refs[block % 2])
        attend_of(block, term_refs[block % 2])
    fetch.wait()


def attend_head(bucket_heads, shared_qk, values, w_out, blocks, bucket_count):
    source_count, tok_rows = bucket_heads.shape
    head_dim = shared_qk.shape[1] // source_count
    token_count = source_count * tok_rows
    query_rows = 2 * tok_rows
    extended = pltpu.VMEM((token_count, 2 * head_dim), shared_qk.dtype)
    scores = pltpu.VMEM((query_rows, token_count), jnp.float32)
    terms = pltpu.VMEM((query_rows, token_count), shared_qk.dtype)
    return pl.pallas_call(
        functools.partial(attend_kernel, bucket_count=bucket_count, query_rows=query_rows),
        in_specs=in_hbm(4) + in_vmem(len(blocks)),
        out_specs=in_vmem(source_count // 2 + 1),
        out_shape=[pltpu.VMEM((2, tok_rows, head_dim), shared_qk.dtype)] * (source_count // 2)
        + [pltpu.VMEM((w_out.shape[0], w_out.shape[1] // 2), w_out.dtype)],
        scratch_shapes=[
            *(extended, extended, extended, scores, scores, terms, terms),
            pltpu.VMEM(bucket_heads.shape, bucket_heads.dtype),
            pltpu.SemaphoreType.DMA((4,)),
        ],
        compiler_params=vmem_params(20),
        name="attend_head",
    )(*(stays_in_hbm(array) for array in (bucket_heads, shared_qk, values, w_out)), *blocks)


def gather_kernel(*refs):
    other = 1 - lax.axis_index("seq") % 2
    for at, pair_ref in enumerate(refs[:-1]):
        refs[-1][at] = pair_ref[other]


def gather_other(pairs):
    _, tok_rows, head_dim = pairs[0].shape
    return pl.pallas_call(
        gather_kernel,
        in_specs=in_vmem(len(pairs)),
        out_specs=in_vmem(1)[0],
        out_shape=pltpu.VMEM((len(pairs), tok_rows, head_dim), pairs[0].dtype),
        compiler_params=vmem_params(8),
        name="gather_other",
    )(*pairs)


def widen_kernel(*refs):
    pair_refs, (swapped_ref, w_ref, out_ref, wide_ref) = refs[:-4], refs[-4:]
    pair_count, _, head_dim = swapped_ref.shape
    own = lax.axis_index("seq")
    for step, pair_ref in enumerate(pair_refs):
        pair = (own // 2 + pair_count - step) % pair_count
        for rows, which in ((pair_ref[own % 2], own % 2), (swapped_ref[step], 1 - own % 2)):
            start = pl.multiple_of((pair * 2 + which) * head_dim, head_dim)
            wide_ref[:, pl.ds(start, head_dim)] = rows
    out_ref[...] = jnp.dot(
        wide_ref[...], w_ref[:, : out_ref.shape[1]], preferred_element_type=jnp.float32
    ).astype(out_ref.dtype)


def widen_and_project(pairs, swapped, w_theirs, columns):
    tok_rows = pairs[0].shape[1]
    return pl.pallas_call(
        widen_kernel,
        in_specs=in_vmem(len(pairs) + 2),
        out_specs=in_vmem(2),
        out_shape=[
            pltpu.VMEM((tok_rows, columns), swapped.dtype),
            pltpu.VMEM((tok_rows, w_theirs.shape[0]), swapped.dtype),
        ],
        compiler_params=vmem_params(16),
        name="widen_and_project",
    )(*pairs, swapped, w_theirs)


def theirs_kernel(wide_ref, w_ref, out_ref, *, start):
    out_ref[...] = jnp.dot(
        wide_ref[...], w_ref[:, start : start + out_ref.shape[1]], preferred_element_type=jnp.float32
    ).astype(out_ref.dtype)


def project_theirs(wide, w_theirs, start):
    return pl.pallas_call(
        functools.partial(theirs_kernel, start=start),
        in_specs=in_vmem(2),
        out_specs=in_vmem(1)[0],
        out_shape=pltpu.VMEM((wide.shape[0], w_theirs.shape[1] - start), wide.dtype),
        compiler_params=vmem_params(16),
        name="project_theirs",
    )(wide, w_theirs)


def ours_kernel(wide_ref, w_hbm, out_ref, w_ref, sems):
    chunks, depth, columns = w_ref.shape
    start = pl.multiple_of(lax.axis_index("mp") * (chunks * columns), columns)
    copies = [
        pltpu.make_async_copy(w_hbm.at[:, pl.ds(start + chunk * columns, columns)], w_ref.at[chunk], sems.at[chunk])
        for chunk in range(chunks)
    ]
    for copy in copies:
        copy.start()
    for chunk, copy in enumerate(copies):
        copy.wait()
        out_ref[:, chunk * columns : (chunk + 1) * columns] = jnp.dot(
            wide_ref[...], w_ref[chunk], preferred_element_type=jnp.float32
        )


def project_ours(wide, w_out):
    tok_rows, depth = wide.shape
    chunks = 4
    columns = w_out.shape[1] // (2 * chunks)
    return pl.pallas_call(
        ours_kernel,
        in_specs=in_vmem(1) + in_hbm(1),
        out_specs=in_vmem(1)[0],
        out_shape=pltpu.VMEM((tok_rows, chunks * columns), jnp.float32),
        scratch_shapes=[
            pltpu.VMEM((chunks, depth, columns), w_out.dtype),
            pltpu.SemaphoreType.DMA((chunks,)),
        ],
        compiler_params=vmem_params(20),
        name="project_ours",
    )(wide, stays_in_hbm(w_out))


def add_kernel(ours_ref, *refs):
    out_ref = refs[-1]
    start = 0
    for theirs_ref in refs[:-1]:
        at = slice(start, start + theirs_ref.shape[1])
        start = at.stop
        out_ref[:, at] = (ours_ref[:, at] + theirs_ref[...].astype(jnp.float32)).astype(out_ref.dtype)


def add_parts(ours, theirs, dtype):
    return pl.pallas_call(
        add_kernel,
        in_specs=in_vmem(1 + len(theirs)),
        out_shape=jax.ShapeDtypeStruct(ours.shape, dtype),
        compiler_params=vmem_params(8),
        name="add_parts",
    )(ours, *theirs)


def local_by_head(shared_qk, values, buckets, counts, w_out):
    bucket_heads = buckets.T
    seq_count = lax.axis_size("seq")
    received = [
        sent(block, step, flip)
        for (step, flip), block in zip(moves(seq_count), pack_blocks(bucket_heads, shared_qk, values))
    ]
    *pairs, w_theirs = attend_head(bucket_heads, shared_qk, values, w_out, received, counts.shape[2])
    pairs = pairs[:1] + [sent(pair, step, 0) for step, pair in enumerate(pairs) if step]
    swapped = sent(gather_other(pairs), 0, 1)
    columns = w_theirs.shape[1] // 4
    first, wide = widen_and_project(pairs, swapped, w_theirs, columns)
    peers = [(0, 1), (1, 0)]
    arrived = [
        lax.ppermute(part, "mp", peers) for part in (first, project_theirs(wide, w_theirs, columns))
    ]
    ours = project_ours(wide, w_out)
    return add_parts(ours, arrived, shared_qk.dtype)


def local(shared_qk, values, buckets, counts, w_out):
    head_count = buckets.shape[1]
    seq_count = lax.axis_size("seq")
    one_head_each = head_count == seq_count and counts.shape[2] == seq_count and 2 < seq_count <= 128 and seq_count % 2 == 0
    if one_head_each and lax.axis_size("mp") == 2 and 2 * shared_qk.shape[0] <= BLOCK:
        return local_by_head(shared_qk, values, buckets, counts, w_out)
    return local_by_bucket(shared_qk, values, buckets, counts, w_out)


def solution(mesh):
    placed = (P("seq", "mp"), P("seq", "mp"), P("seq", "mp"), P(None, "mp", None), P("mp", None))
    return jax.shard_map(
        local, mesh=mesh, in_specs=placed, out_specs=P("seq", "mp"), check_vma=False
    )
```

```python
import functools
import math

import jax
import jax.numpy as jnp
from jax import lax
from jax.experimental import pallas as pl
from jax.experimental.pallas import tpu as pltpu
from jax.sharding import PartitionSpec as P


BLOCK = 256
MASKED = -1e30


SELF_SCORE = -100000.0


def passed_along(shard, axis, by):
    devices = lax.axis_size(axis)
    return lax.ppermute(shard, axis, [(i, (i + by) % devices) for i in range(devices)])


def block_attention(queries, window, window_live):
    head_dim = queries.shape[-1]
    block_rows = queries.shape[-2]
    key_rows = window[..., :head_dim]
    value_rows = window[..., head_dim:]
    scores = jnp.einsum("cqd,ckd->cqk", queries, key_rows, preferred_element_type=jnp.float32) * (
        1.0 / math.sqrt(head_dim)
    )
    query_place = jnp.arange(block_rows)[:, None] + block_rows
    key_place = jnp.arange(2 * block_rows)[None, :]
    itself = query_place == key_place
    scores = jnp.where(itself[None], SELF_SCORE, scores)
    allowed = window_live[:, None, :] | itself[None]
    row_max = jnp.max(jnp.where(allowed, scores, -1e30), axis=-1, keepdims=True)
    exp_terms = jnp.where(allowed, jnp.exp(scores - row_max), 0.0)
    weights = (exp_terms / jnp.sum(exp_terms, axis=-1, keepdims=True)).astype(jnp.bfloat16)
    attended = jnp.einsum("cqk,ckd->cqd", weights, value_rows, preferred_element_type=jnp.float32)
    return attended.astype(jnp.bfloat16)


def owner_layout(received, column, slot_count):
    source_count = column.shape[0]
    head_count = column.shape[1]
    upto_count = jnp.cumsum(column, axis=0)
    before_count = upto_count - column
    bucket_total = upto_count[-1]
    slot_range = jnp.arange(slot_count)
    source_dev = jnp.sum(upto_count[:, :, None] <= slot_range[None, None, :], axis=0)
    source_dev = jnp.minimum(source_dev, source_count - 1)
    source_range = jnp.arange(source_count)
    source_start = jnp.sum(
        jnp.where(source_dev[None] == source_range[:, None, None], before_count[:, :, None], 0),
        axis=0,
    )
    entry_row = jnp.clip(slot_range[None, :] - source_start, 0, received.shape[2] - 1)
    head_range = jnp.arange(head_count)
    layout = received[source_dev, head_range[:, None], entry_row]
    live = slot_range[None, :] < bucket_total[:, None]
    layout = jnp.where(live[..., None], layout, jnp.zeros((), layout.dtype))
    return (layout, live, before_count, bucket_total)


def tail_live(bucket_total, block_rows):
    return bucket_total[:, None] - block_rows + jnp.arange(block_rows)[None, :] >= 0


def last_rows(layout, bucket_total, block_rows):
    rank_index = bucket_total[:, None] - block_rows + jnp.arange(block_rows)[None, :]
    head_range = jnp.arange(layout.shape[0])
    rows = layout[head_range[:, None], jnp.maximum(rank_index, 0)]
    return jnp.where((rank_index >= 0)[..., None], rows, jnp.zeros((), rows.dtype))


def local_by_bucket(shared_qk, values, buckets, counts, w_out):
    tok_rows = shared_qk.shape[0]
    head_count = buckets.shape[1]
    head_dim = shared_qk.shape[1] // head_count
    seq_count = lax.axis_size("seq")
    capacity = 2 * tok_rows // seq_count
    slot_count = seq_count * capacity
    block_rows = BLOCK
    block_count = slot_count // block_rows
    own_index = lax.axis_index("seq")
    prev_index = (own_index + seq_count - 1) % seq_count
    head_range = jnp.arange(head_count)
    bucket_heads = buckets.T
    positions = jnp.arange(tok_rows)
    earlier = positions[None, :] < positions[:, None]
    same_bucket = bucket_heads[:, :, None] == bucket_heads[:, None, :]
    within = jnp.sum(same_bucket & earlier[None], axis=2)
    own_counts = lax.dynamic_index_in_dim(counts, own_index, 0, keepdims=False)
    own_starts = jnp.cumsum(own_counts, axis=1) - own_counts
    bucket_range = jnp.arange(seq_count)
    one_hot = bucket_heads[:, :, None] == bucket_range[None, None, :]
    token_start = jnp.sum(jnp.where(one_hot, own_starts[:, None, :], 0), axis=2)
    sorted_pos = token_start + within
    token_order = jnp.sum(
        jnp.where(sorted_pos[:, :, None] == positions[None, None, :], positions[None, :, None], 0),
        axis=1,
    )
    slot_range = jnp.arange(capacity)
    send_index = own_starts.T[:, :, None] + slot_range[None, None, :]
    filled = slot_range[None, None, :] < own_counts.T[:, :, None]
    token_pick = token_order[head_range[None, :, None], jnp.minimum(send_index, tok_rows - 1)]
    packed = jnp.concatenate(
        [
            shared_qk.reshape(tok_rows, head_count, head_dim),
            values.reshape(tok_rows, head_count, head_dim),
        ],
        axis=2,
    )
    outgoing = packed[token_pick, head_range[None, :, None]]
    outgoing = jnp.where(filled[..., None], outgoing, jnp.zeros((), outgoing.dtype))
    own_column = lax.dynamic_index_in_dim(counts, own_index, 2, keepdims=False)
    prev_column = lax.dynamic_index_in_dim(counts, prev_index, 2, keepdims=False)
    prev_total = jnp.sum(prev_column, axis=0)
    received = lax.all_to_all(outgoing, "seq", split_axis=0, concat_axis=0, tiled=True)
    layout, live, before_count, bucket_total = owner_layout(received, own_column, slot_count)
    tail_rows = last_rows(layout, bucket_total, block_rows)
    prev_rows = passed_along(tail_rows, "seq", 1)
    prev_live = tail_live(prev_total, block_rows)
    keys_all = jnp.concatenate([prev_rows, layout], axis=1)
    live_all = jnp.concatenate([prev_live, live], axis=1)
    window = jnp.concatenate(
        [
            keys_all[:, :slot_count].reshape(head_count, block_count, block_rows, 2 * head_dim),
            keys_all[:, block_rows:].reshape(head_count, block_count, block_rows, 2 * head_dim),
        ],
        axis=2,
    )
    window_live = jnp.concatenate(
        [
            live_all[:, :slot_count].reshape(head_count, block_count, block_rows),
            live_all[:, block_rows:].reshape(head_count, block_count, block_rows),
        ],
        axis=2,
    )
    queries = layout[..., :head_dim].reshape(head_count, block_count, block_rows, head_dim)
    attended = lax.map(
        lambda per_head: block_attention(per_head[0], per_head[1], per_head[2]),
        (queries, window, window_live),
    )
    out_layout = attended.reshape(head_count, slot_count, head_dim)
    back_index = before_count[:, :, None] + slot_range[None, None, :]
    back_filled = slot_range[None, None, :] < own_column[:, :, None]
    back_rows = out_layout[head_range[None, :, None], jnp.minimum(back_index, slot_count - 1)]
    back_rows = jnp.where(back_filled[..., None], back_rows, jnp.zeros((), back_rows.dtype))
    returned = lax.all_to_all(back_rows, "seq", split_axis=0, concat_axis=0, tiled=True)
    token_out = returned[buckets, head_range[None, :], within.T]
    token_out = token_out.reshape(tok_rows, head_count * head_dim)
    partial_sum = jnp.dot(token_out, w_out, preferred_element_type=jnp.float32)
    projected = lax.psum_scatter(partial_sum, "mp", scatter_dimension=1, tiled=True)
    return projected.astype(jnp.bfloat16)


PAD_ROWS = 8


def in_vmem(count):
    return [pl.BlockSpec(memory_space=pltpu.VMEM)] * count


def in_hbm(count):
    return [pl.BlockSpec(memory_space=pltpu.HBM)] * count


def stays_in_hbm(array):
    return pltpu.with_memory_space_constraint(array, pltpu.HBM)


def vmem_params(mebibytes):
    return pltpu.CompilerParams(vmem_limit_bytes=mebibytes * 2**20)


def moves(count):
    every = [(step, flip) for step in range(count // 2) for flip in range(2)]
    return sorted(every[1:], key=lambda move: (move[0] % 2, move[1], move[0]))


def moved(index, step, flip, count):
    return (index // 2 + step) % (count // 2) * 2 + (index % 2 + flip) % 2


def sent(block, step, flip):
    count = lax.axis_size("seq")
    return lax.ppermute(block, "seq", [(i, moved(i, step, flip, count)) for i in range(count)])


def block_copies(qk_hbm, value_hbm, head, qk_ref, value_ref, sems):
    head_dim = qk_ref.shape[1]
    columns = pl.ds(pl.multiple_of(head * head_dim, head_dim), head_dim)
    return [
        pltpu.make_async_copy(qk_hbm.at[:, columns], qk_ref, sems.at[0]),
        pltpu.make_async_copy(value_hbm.at[:, columns], value_ref, sems.at[1]),
    ]


def pack_kernel(bucket_hbm, qk_hbm, value_hbm, *refs):
    outs, (bucket_ref, bucket_sem, sems) = refs[:-3], refs[-3:]
    head_count = bucket_ref.shape[0]
    tok_rows = qk_hbm.shape[0]
    own = lax.axis_index("seq")
    heads = [moved(own, step, flip, head_count) for step, flip in moves(head_count)]
    fetch_buckets = pltpu.make_async_copy(bucket_hbm, bucket_ref, bucket_sem)
    fetch_buckets.start()
    copies = []
    for at, (head, out) in enumerate(zip(heads, outs)):
        qk_ref, value_ref = out.at[:tok_rows, :], out.at[tok_rows : 2 * tok_rows, :]
        copies += block_copies(qk_hbm, value_hbm, head, qk_ref, value_ref, sems.at[at])
    for copy in copies:
        copy.start()
    fetch_buckets.wait()
    for head, out in zip(heads, outs):
        bucket = bucket_ref[pl.ds(head, 1), :].astype(jnp.float32)
        out[2 * tok_rows :, :] = jnp.broadcast_to(bucket, (PAD_ROWS, tok_rows)).astype(out.dtype)
    for copy in copies:
        copy.wait()


def pack_blocks(bucket_heads, shared_qk, values):
    head_count, tok_rows = bucket_heads.shape
    head_dim = shared_qk.shape[1] // head_count
    block = pltpu.VMEM((2 * tok_rows + PAD_ROWS, head_dim), shared_qk.dtype)
    return pl.pallas_call(
        pack_kernel,
        in_specs=in_hbm(3),
        out_specs=in_vmem(head_count - 1),
        out_shape=[block] * (head_count - 1),
        scratch_shapes=[
            pltpu.VMEM(bucket_heads.shape, bucket_heads.dtype),
            pltpu.SemaphoreType.DMA(()),
            pltpu.SemaphoreType.DMA((head_count - 1, 2)),
        ],
        compiler_params=vmem_params(8),
        name="pack_blocks",
    )(*(stays_in_hbm(array) for array in (bucket_heads, shared_qk, values)))


def attend_kernel(bucket_hbm, qk_hbm, value_hbm, w_hbm, *refs, bucket_count, query_rows):
    source_count = bucket_hbm.shape[0]
    pair_count = source_count // 2
    block_refs, refs = refs[: source_count - 1], refs[source_count - 1 :]
    out_refs, refs = refs[:pair_count], refs[pair_count:]
    w_ref, query_ref, key_ref, value_ref = refs[:4]
    score_refs, term_refs = refs[4:7], refs[7:9]
    bucket_ref, sems = refs[9:]
    _, tok_rows, head_dim = out_refs[0].shape
    token_count = source_count * tok_rows
    own = lax.axis_index("seq")
    owners = [(-step % pair_count, (own + flip) % 2) for step, flip in (*moves(source_count), (0, 0))]
    last = slice(token_count - tok_rows, token_count)
    own_copies = block_copies(qk_hbm, value_hbm, own, key_ref.at[last, :head_dim], value_ref.at[last, :head_dim], sems)
    own_copies.append(pltpu.make_async_copy(bucket_hbm, bucket_ref, sems.at[2]))
    for copy in own_copies:
        copy.start()
    width = w_ref.shape[1]
    theirs = pl.multiple_of((1 - lax.axis_index("mp")) * width, width)
    fetch = pltpu.make_async_copy(w_hbm.at[:, pl.ds(theirs, width)], w_ref, sems.at[3])
    fetch.start()
    lane = lax.broadcasted_iota(jnp.int32, (tok_rows, head_dim), 1)

    def prepare(source):
        at = slice(source * tok_rows, (source + 1) * tok_rows)
        if source < source_count - 1:
            block_ref = block_refs[source]
            query_ref[at, :head_dim] = block_ref[:tok_rows, :]
            key_ref[at, :head_dim] = block_ref[:tok_rows, :]
            value_ref[at, :head_dim] = block_ref[tok_rows : 2 * tok_rows, :]
            row = block_ref[2 * tok_rows :, :].astype(jnp.float32)[:1]
        else:
            for copy in own_copies:
                copy.wait()
            query_ref[at, :head_dim] = key_ref[at, :head_dim]
            row = bucket_ref[pl.ds(own, 1), :].astype(jnp.float32)
        value_ref[at, head_dim:] = jnp.ones((tok_rows, head_dim), value_ref.dtype)
        bucket = jnp.broadcast_to(row, (head_dim, tok_rows)).T.astype(jnp.int32)
        following = jnp.where(bucket == bucket_count - 1, 0, bucket + 1)
        same = lane == bucket
        query_ref[at, head_dim:] = jnp.where(same, 1.0, 0.0).astype(query_ref.dtype)
        key_ref[at, head_dim:] = jnp.where(same | (lane == following), 0.0, MASKED).astype(key_ref.dtype)

    scale = 1.0 / math.sqrt(head_dim)
    strip = 16
    square = (tok_rows, tok_rows)
    itself = lax.broadcasted_iota(jnp.int32, square, 0) == lax.broadcasted_iota(jnp.int32, square, 1)

    def scores_of(block, score_ref, keys):
        score_ref[:, keys] = lax.dot_general(
            query_ref[block * query_rows : (block + 1) * query_rows, :],
            key_ref[keys, :],
            (((1,), (1,)), ((), ())),
            preferred_element_type=jnp.float32,
        )

    def replace_diagonal(block, score_ref):
        for at in range(0, query_rows, tok_rows):
            columns = slice(block * query_rows + at, block * query_rows + at + tok_rows)
            diagonal = score_ref[at : at + tok_rows, columns]
            score_ref[at : at + tok_rows, columns] = jnp.where(itself, SELF_SCORE / scale, diagonal)

    def terms_of(score_ref, term_ref):
        for at in range(0, query_rows, strip):
            scores = score_ref[at : at + strip, :]
            row_max = jnp.max(scores, axis=1, keepdims=True)
            terms = jnp.exp2((scores - row_max) * (scale * math.log2(math.e)))
            term_ref[at : at + strip, :] = terms.astype(term_ref.dtype)

    def attend_of(block, term_ref):
        both = jnp.dot(term_ref[...], value_ref[...], preferred_element_type=jnp.float32)
        attended = (both[:, :head_dim] / both[:, head_dim:]).astype(out_refs[0].dtype)
        for at in range(0, query_rows, tok_rows):
            step, which = owners[(block * query_rows + at) // tok_rows]
            out_refs[step][which] = attended[at : at + tok_rows]

    blocks = token_count // query_rows
    ahead = min(2, blocks)
    for tile in range(blocks):
        stop = (tile + 1) * query_rows
        for source in range(tile * query_rows // tok_rows, stop // tok_rows):
            prepare(source)
        for block in range(min(tile + 1, ahead)):
            keys = slice(0 if tile == block else tile * query_rows, stop)
            scores_of(block, score_refs[block], keys)
    for block in range(ahead):
        replace_diagonal(block, score_refs[block])
    for block in range(blocks):
        if block + ahead < blocks:
            scores_of(block + ahead, score_refs[(block + ahead) % 3], slice(0, token_count))
            replace_diagonal(block + ahead, score_refs[(block + ahead) % 3])
        terms_of(score_refs[block % 3], term_refs[block % 2])
        attend_of(block, term_refs[block % 2])
    fetch.wait()


def attend_head(bucket_heads, shared_qk, values, w_out, blocks, bucket_count):
    source_count, tok_rows = bucket_heads.shape
    head_dim = shared_qk.shape[1] // source_count
    token_count = source_count * tok_rows
    query_rows = 2 * tok_rows
    extended = pltpu.VMEM((token_count, 2 * head_dim), shared_qk.dtype)
    scores = pltpu.VMEM((query_rows, token_count), jnp.float32)
    terms = pltpu.VMEM((query_rows, token_count), shared_qk.dtype)
    return pl.pallas_call(
        functools.partial(attend_kernel, bucket_count=bucket_count, query_rows=query_rows),
        in_specs=in_hbm(4) + in_vmem(len(blocks)),
        out_specs=in_vmem(source_count // 2 + 1),
        out_shape=[pltpu.VMEM((2, tok_rows, head_dim), shared_qk.dtype)] * (source_count // 2)
        + [pltpu.VMEM((w_out.shape[0], w_out.shape[1] // 2), w_out.dtype)],
        scratch_shapes=[
            *(extended, extended, extended, scores, scores, scores, terms, terms),
            pltpu.VMEM(bucket_heads.shape, bucket_heads.dtype),
            pltpu.SemaphoreType.DMA((4,)),
        ],
        compiler_params=vmem_params(20),
        name="attend_head",
    )(*(stays_in_hbm(array) for array in (bucket_heads, shared_qk, values, w_out)), *blocks)


def gather_kernel(*refs):
    other = 1 - lax.axis_index("seq") % 2
    for at, pair_ref in enumerate(refs[:-1]):
        refs[-1][at] = pair_ref[other]


def gather_other(pairs):
    _, tok_rows, head_dim = pairs[0].shape
    return pl.pallas_call(
        gather_kernel,
        in_specs=in_vmem(len(pairs)),
        out_specs=in_vmem(1)[0],
        out_shape=pltpu.VMEM((len(pairs), tok_rows, head_dim), pairs[0].dtype),
        compiler_params=vmem_params(8),
        name="gather_other",
    )(*pairs)


def widen_kernel(*refs):
    pair_refs, (swapped_ref, w_ref, out_ref, wide_ref) = refs[:-4], refs[-4:]
    pair_count, _, head_dim = swapped_ref.shape
    own = lax.axis_index("seq")
    for step, pair_ref in enumerate(pair_refs):
        pair = (own // 2 + pair_count - step) % pair_count
        for rows, which in ((pair_ref[own % 2], own % 2), (swapped_ref[step], 1 - own % 2)):
            start = pl.multiple_of((pair * 2 + which) * head_dim, head_dim)
            wide_ref[:, pl.ds(start, head_dim)] = rows
    out_ref[...] = jnp.dot(
        wide_ref[...], w_ref[:, : out_ref.shape[1]], preferred_element_type=jnp.float32
    ).astype(out_ref.dtype)


def widen_and_project(pairs, swapped, w_theirs, columns):
    tok_rows = pairs[0].shape[1]
    return pl.pallas_call(
        widen_kernel,
        in_specs=in_vmem(len(pairs) + 2),
        out_specs=in_vmem(2),
        out_shape=[
            pltpu.VMEM((tok_rows, columns), swapped.dtype),
            pltpu.VMEM((tok_rows, w_theirs.shape[0]), swapped.dtype),
        ],
        compiler_params=vmem_params(16),
        name="widen_and_project",
    )(*pairs, swapped, w_theirs)


def theirs_kernel(wide_ref, w_ref, out_ref, *, start):
    out_ref[...] = jnp.dot(
        wide_ref[...], w_ref[:, start : start + out_ref.shape[1]], preferred_element_type=jnp.float32
    ).astype(out_ref.dtype)


def project_theirs(wide, w_theirs, start):
    return pl.pallas_call(
        functools.partial(theirs_kernel, start=start),
        in_specs=in_vmem(2),
        out_specs=in_vmem(1)[0],
        out_shape=pltpu.VMEM((wide.shape[0], w_theirs.shape[1] - start), wide.dtype),
        compiler_params=vmem_params(16),
        name="project_theirs",
    )(wide, w_theirs)


def ours_kernel(wide_ref, w_hbm, out_ref, w_ref, sems):
    chunks, _, columns = w_ref.shape
    start = pl.multiple_of(lax.axis_index("mp") * (chunks * columns), columns)
    copies = [
        pltpu.make_async_copy(w_hbm.at[:, pl.ds(start + chunk * columns, columns)], w_ref.at[chunk], sems.at[chunk])
        for chunk in range(chunks)
    ]
    for copy in copies:
        copy.start()
    for chunk, copy in enumerate(copies):
        copy.wait()
        out_ref[:, chunk * columns : (chunk + 1) * columns] = jnp.dot(
            wide_ref[...], w_ref[chunk], preferred_element_type=jnp.float32
        )


def project_ours(wide, w_out):
    tok_rows, depth = wide.shape
    chunks = 4
    columns = w_out.shape[1] // (2 * chunks)
    return pl.pallas_call(
        ours_kernel,
        in_specs=in_vmem(1) + in_hbm(1),
        out_specs=in_vmem(1)[0],
        out_shape=pltpu.VMEM((tok_rows, chunks * columns), jnp.float32),
        scratch_shapes=[
            pltpu.VMEM((chunks, depth, columns), w_out.dtype),
            pltpu.SemaphoreType.DMA((chunks,)),
        ],
        compiler_params=vmem_params(20),
        name="project_ours",
    )(wide, stays_in_hbm(w_out))


def add_kernel(ours_ref, *refs):
    out_ref = refs[-1]
    start = 0
    for theirs_ref in refs[:-1]:
        at = slice(start, start + theirs_ref.shape[1])
        start = at.stop
        out_ref[:, at] = (ours_ref[:, at] + theirs_ref[...].astype(jnp.float32)).astype(out_ref.dtype)


def add_parts(ours, theirs, dtype):
    return pl.pallas_call(
        add_kernel,
        in_specs=in_vmem(1 + len(theirs)),
        out_shape=jax.ShapeDtypeStruct(ours.shape, dtype),
        compiler_params=vmem_params(8),
        name="add_parts",
    )(ours, *theirs)


def local_by_head(shared_qk, values, buckets, counts, w_out):
    bucket_heads = buckets.T
    seq_count = lax.axis_size("seq")
    received = [
        sent(block, step, flip)
        for (step, flip), block in zip(moves(seq_count), pack_blocks(bucket_heads, shared_qk, values))
    ]
    *pairs, w_theirs = attend_head(bucket_heads, shared_qk, values, w_out, received, counts.shape[2])
    pairs = pairs[:1] + [sent(pair, step, 0) for step, pair in enumerate(pairs) if step]
    swapped = sent(gather_other(pairs), 0, 1)
    columns = w_theirs.shape[1] // 4
    first, wide = widen_and_project(pairs, swapped, w_theirs, columns)
    peers = [(0, 1), (1, 0)]
    arrived = [lax.ppermute(first, "mp", peers)]
    rest = project_theirs(wide, w_theirs, columns)
    arrived.append(lax.ppermute(rest, "mp", peers))
    ours = project_ours(wide, w_out)
    return add_parts(ours, arrived, shared_qk.dtype)


def local(shared_qk, values, buckets, counts, w_out):
    head_count = buckets.shape[1]
    seq_count = lax.axis_size("seq")
    one_head_each = head_count == seq_count and counts.shape[2] == seq_count and 2 < seq_count <= 128 and seq_count % 2 == 0
    if one_head_each and lax.axis_size("mp") == 2 and 2 * shared_qk.shape[0] <= BLOCK:
        return local_by_head(shared_qk, values, buckets, counts, w_out)
    return local_by_bucket(shared_qk, values, buckets, counts, w_out)


def solution(mesh):
    placed = (P("seq", "mp"), P("seq", "mp"), P("seq", "mp"), P(None, "mp", None), P("mp", None))
    return jax.shard_map(
        local, mesh=mesh, in_specs=placed, out_specs=P("seq", "mp"), check_vma=False
    )
```

```python
import functools
import math

import jax
import jax.numpy as jnp
from jax import lax
from jax.experimental import pallas as pl
from jax.experimental.pallas import tpu as pltpu
from jax.sharding import PartitionSpec as P


BLOCK = 256
MASKED = -1e30


SELF_SCORE = -100000.0


def passed_along(shard, axis, by):
    devices = lax.axis_size(axis)
    return lax.ppermute(shard, axis, [(i, (i + by) % devices) for i in range(devices)])


def block_attention(queries, window, window_live):
    head_dim = queries.shape[-1]
    block_rows = queries.shape[-2]
    key_rows = window[..., :head_dim]
    value_rows = window[..., head_dim:]
    scores = jnp.einsum("cqd,ckd->cqk", queries, key_rows, preferred_element_type=jnp.float32) * (
        1.0 / math.sqrt(head_dim)
    )
    query_place = jnp.arange(block_rows)[:, None] + block_rows
    key_place = jnp.arange(2 * block_rows)[None, :]
    itself = query_place == key_place
    scores = jnp.where(itself[None], SELF_SCORE, scores)
    allowed = window_live[:, None, :] | itself[None]
    row_max = jnp.max(jnp.where(allowed, scores, -1e30), axis=-1, keepdims=True)
    exp_terms = jnp.where(allowed, jnp.exp(scores - row_max), 0.0)
    weights = (exp_terms / jnp.sum(exp_terms, axis=-1, keepdims=True)).astype(jnp.bfloat16)
    attended = jnp.einsum("cqk,ckd->cqd", weights, value_rows, preferred_element_type=jnp.float32)
    return attended.astype(jnp.bfloat16)


def owner_layout(received, column, slot_count):
    source_count = column.shape[0]
    head_count = column.shape[1]
    upto_count = jnp.cumsum(column, axis=0)
    before_count = upto_count - column
    bucket_total = upto_count[-1]
    slot_range = jnp.arange(slot_count)
    source_dev = jnp.sum(upto_count[:, :, None] <= slot_range[None, None, :], axis=0)
    source_dev = jnp.minimum(source_dev, source_count - 1)
    source_range = jnp.arange(source_count)
    source_start = jnp.sum(
        jnp.where(source_dev[None] == source_range[:, None, None], before_count[:, :, None], 0),
        axis=0,
    )
    entry_row = jnp.clip(slot_range[None, :] - source_start, 0, received.shape[2] - 1)
    head_range = jnp.arange(head_count)
    layout = received[source_dev, head_range[:, None], entry_row]
    live = slot_range[None, :] < bucket_total[:, None]
    layout = jnp.where(live[..., None], layout, jnp.zeros((), layout.dtype))
    return (layout, live, before_count, bucket_total)


def tail_live(bucket_total, block_rows):
    return bucket_total[:, None] - block_rows + jnp.arange(block_rows)[None, :] >= 0


def last_rows(layout, bucket_total, block_rows):
    rank_index = bucket_total[:, None] - block_rows + jnp.arange(block_rows)[None, :]
    head_range = jnp.arange(layout.shape[0])
    rows = layout[head_range[:, None], jnp.maximum(rank_index, 0)]
    return jnp.where((rank_index >= 0)[..., None], rows, jnp.zeros((), rows.dtype))


def local_by_bucket(shared_qk, values, buckets, counts, w_out):
    tok_rows = shared_qk.shape[0]
    head_count = buckets.shape[1]
    head_dim = shared_qk.shape[1] // head_count
    seq_count = lax.axis_size("seq")
    capacity = 2 * tok_rows // seq_count
    slot_count = seq_count * capacity
    block_rows = BLOCK
    block_count = slot_count // block_rows
    own_index = lax.axis_index("seq")
    prev_index = (own_index + seq_count - 1) % seq_count
    head_range = jnp.arange(head_count)
    bucket_heads = buckets.T
    positions = jnp.arange(tok_rows)
    earlier = positions[None, :] < positions[:, None]
    same_bucket = bucket_heads[:, :, None] == bucket_heads[:, None, :]
    within = jnp.sum(same_bucket & earlier[None], axis=2)
    own_counts = lax.dynamic_index_in_dim(counts, own_index, 0, keepdims=False)
    own_starts = jnp.cumsum(own_counts, axis=1) - own_counts
    bucket_range = jnp.arange(seq_count)
    one_hot = bucket_heads[:, :, None] == bucket_range[None, None, :]
    token_start = jnp.sum(jnp.where(one_hot, own_starts[:, None, :], 0), axis=2)
    sorted_pos = token_start + within
    token_order = jnp.sum(
        jnp.where(sorted_pos[:, :, None] == positions[None, None, :], positions[None, :, None], 0),
        axis=1,
    )
    slot_range = jnp.arange(capacity)
    send_index = own_starts.T[:, :, None] + slot_range[None, None, :]
    filled = slot_range[None, None, :] < own_counts.T[:, :, None]
    token_pick = token_order[head_range[None, :, None], jnp.minimum(send_index, tok_rows - 1)]
    packed = jnp.concatenate(
        [
            shared_qk.reshape(tok_rows, head_count, head_dim),
            values.reshape(tok_rows, head_count, head_dim),
        ],
        axis=2,
    )
    outgoing = packed[token_pick, head_range[None, :, None]]
    outgoing = jnp.where(filled[..., None], outgoing, jnp.zeros((), outgoing.dtype))
    own_column = lax.dynamic_index_in_dim(counts, own_index, 2, keepdims=False)
    prev_column = lax.dynamic_index_in_dim(counts, prev_index, 2, keepdims=False)
    prev_total = jnp.sum(prev_column, axis=0)
    received = lax.all_to_all(outgoing, "seq", split_axis=0, concat_axis=0, tiled=True)
    layout, live, before_count, bucket_total = owner_layout(received, own_column, slot_count)
    tail_rows = last_rows(layout, bucket_total, block_rows)
    prev_rows = passed_along(tail_rows, "seq", 1)
    prev_live = tail_live(prev_total, block_rows)
    keys_all = jnp.concatenate([prev_rows, layout], axis=1)
    live_all = jnp.concatenate([prev_live, live], axis=1)
    window = jnp.concatenate(
        [
            keys_all[:, :slot_count].reshape(head_count, block_count, block_rows, 2 * head_dim),
            keys_all[:, block_rows:].reshape(head_count, block_count, block_rows, 2 * head_dim),
        ],
        axis=2,
    )
    window_live = jnp.concatenate(
        [
            live_all[:, :slot_count].reshape(head_count, block_count, block_rows),
            live_all[:, block_rows:].reshape(head_count, block_count, block_rows),
        ],
        axis=2,
    )
    queries = layout[..., :head_dim].reshape(head_count, block_count, block_rows, head_dim)
    attended = lax.map(
        lambda per_head: block_attention(per_head[0], per_head[1], per_head[2]),
        (queries, window, window_live),
    )
    out_layout = attended.reshape(head_count, slot_count, head_dim)
    back_index = before_count[:, :, None] + slot_range[None, None, :]
    back_filled = slot_range[None, None, :] < own_column[:, :, None]
    back_rows = out_layout[head_range[None, :, None], jnp.minimum(back_index, slot_count - 1)]
    back_rows = jnp.where(back_filled[..., None], back_rows, jnp.zeros((), back_rows.dtype))
    returned = lax.all_to_all(back_rows, "seq", split_axis=0, concat_axis=0, tiled=True)
    token_out = returned[buckets, head_range[None, :], within.T]
    token_out = token_out.reshape(tok_rows, head_count * head_dim)
    partial_sum = jnp.dot(token_out, w_out, preferred_element_type=jnp.float32)
    projected = lax.psum_scatter(partial_sum, "mp", scatter_dimension=1, tiled=True)
    return projected.astype(jnp.bfloat16)


PAD_ROWS = 8
FETCHES = 8


def in_vmem(count):
    return [pl.BlockSpec(memory_space=pltpu.VMEM)] * count


def in_hbm(count):
    return [pl.BlockSpec(memory_space=pltpu.HBM)] * count


def stays_in_hbm(array):
    return pltpu.with_memory_space_constraint(array, pltpu.HBM)


def vmem_params(mebibytes):
    return pltpu.CompilerParams(vmem_limit_bytes=mebibytes * 2**20)


def moves(count):
    every = [(step, flip) for step in range(count // 2) for flip in range(2)]
    return sorted(every[1:], key=lambda move: (move[0] % 2, move[1], move[0]))


def moved(index, step, flip, count):
    return (index // 2 + step) % (count // 2) * 2 + (index % 2 + flip) % 2


def sent(block, step, flip):
    count = lax.axis_size("seq")
    return lax.ppermute(block, "seq", [(i, moved(i, step, flip, count)) for i in range(count)])


def block_copies(qk_hbm, value_hbm, head, qk_ref, value_ref, sems):
    head_dim = qk_ref.shape[1]
    columns = pl.ds(pl.multiple_of(head * head_dim, head_dim), head_dim)
    return [
        pltpu.make_async_copy(qk_hbm.at[:, columns], qk_ref, sems.at[0]),
        pltpu.make_async_copy(value_hbm.at[:, columns], value_ref, sems.at[1]),
    ]


def pack_kernel(bucket_hbm, qk_hbm, value_hbm, *refs):
    outs, (bucket_ref, bucket_sem, sems) = refs[:-3], refs[-3:]
    head_count = bucket_ref.shape[0]
    tok_rows = qk_hbm.shape[0]
    own = lax.axis_index("seq")
    heads = [moved(own, step, flip, head_count) for step, flip in moves(head_count)]
    fetch_buckets = pltpu.make_async_copy(bucket_hbm, bucket_ref, bucket_sem)
    fetch_buckets.start()
    copies = []
    for at, (head, out) in enumerate(zip(heads, outs)):
        qk_ref, value_ref = out.at[:tok_rows, :], out.at[tok_rows : 2 * tok_rows, :]
        copies += block_copies(qk_hbm, value_hbm, head, qk_ref, value_ref, sems.at[at])
    for copy in copies:
        copy.start()
    fetch_buckets.wait()
    for head, out in zip(heads, outs):
        bucket = bucket_ref[pl.ds(head, 1), :].astype(jnp.float32)
        out[2 * tok_rows :, :] = jnp.broadcast_to(bucket, (PAD_ROWS, tok_rows)).astype(out.dtype)
    for copy in copies:
        copy.wait()


def pack_blocks(bucket_heads, shared_qk, values):
    head_count, tok_rows = bucket_heads.shape
    head_dim = shared_qk.shape[1] // head_count
    block = pltpu.VMEM((2 * tok_rows + PAD_ROWS, head_dim), shared_qk.dtype)
    return pl.pallas_call(
        pack_kernel,
        in_specs=in_hbm(3),
        out_specs=in_vmem(head_count - 1),
        out_shape=[block] * (head_count - 1),
        scratch_shapes=[
            pltpu.VMEM(bucket_heads.shape, bucket_heads.dtype),
            pltpu.SemaphoreType.DMA(()),
            pltpu.SemaphoreType.DMA((head_count - 1, 2)),
        ],
        compiler_params=vmem_params(8),
        name="pack_blocks",
    )(*(stays_in_hbm(array) for array in (bucket_heads, shared_qk, values)))


def extend(block, bucket_row, query_ref, key_ref, value_ref, rows, bucket_count):
    qk, value = block
    tok_rows, head_dim = value.shape
    lane = lax.broadcasted_iota(jnp.int32, (tok_rows, head_dim), 1)
    query_ref[rows, :head_dim] = qk
    key_ref[rows, :head_dim] = qk
    value_ref[rows, :head_dim] = value
    value_ref[rows, head_dim:] = jnp.ones((tok_rows, head_dim), value_ref.dtype)
    bucket = jnp.broadcast_to(bucket_row, (head_dim, tok_rows)).T.astype(jnp.int32)
    following = jnp.where(bucket == bucket_count - 1, 0, bucket + 1)
    same = lane == bucket
    query_ref[rows, head_dim:] = jnp.where(same, 1.0, 0.0).astype(query_ref.dtype)
    key_ref[rows, head_dim:] = jnp.where(same | (lane == following), 0.0, MASKED).astype(key_ref.dtype)


def extend_received(block_ref, query_ref, key_ref, value_ref, rows, bucket_count):
    tok_rows = (block_ref.shape[0] - PAD_ROWS) // 2
    block = (block_ref[:tok_rows, :], block_ref[tok_rows : 2 * tok_rows, :])
    bucket_row = block_ref[2 * tok_rows :, :].astype(jnp.float32)[:1]
    extend(block, bucket_row, query_ref, key_ref, value_ref, rows, bucket_count)


def products(queries, keys):
    return lax.dot_general(queries, keys, (((1,), (1,)), ((), ())), preferred_element_type=jnp.float32)


def replace_diagonal(score_ref, start, size, head_dim):
    square = (size, size)
    itself = lax.broadcasted_iota(jnp.int32, square, 0) == lax.broadcasted_iota(jnp.int32, square, 1)
    replaced = SELF_SCORE * math.sqrt(head_dim)
    for at in range(0, score_ref.shape[0], size):
        columns = slice(start + at, start + at + size)
        diagonal = score_ref[at : at + size, columns]
        score_ref[at : at + size, columns] = jnp.where(itself, replaced, diagonal)


def early_kernel(bucket_hbm, qk_hbm, value_hbm, *refs, bucket_count):
    refs, (bucket_ref, own_qk_ref, own_value_ref, sems) = refs[:-4], refs[-4:]
    block_refs, (query_ref, key_ref, value_ref, *score_refs) = refs[:-5], refs[-5:]
    tok_rows, head_dim = own_qk_ref.shape
    query_rows = score_refs[0].shape[0]
    own = lax.axis_index("seq")
    copies = block_copies(qk_hbm, value_hbm, own, own_qk_ref, own_value_ref, sems)
    copies.append(pltpu.make_async_copy(bucket_hbm, bucket_ref, sems.at[2]))
    for copy in copies:
        copy.start()
    for at, block_ref in enumerate(block_refs):
        rows = slice((at + 1) * tok_rows, (at + 2) * tok_rows)
        extend_received(block_ref, query_ref, key_ref, value_ref, rows, bucket_count)
    early = slice(0, (len(block_refs) + 1) * tok_rows)
    for copy in copies:
        copy.wait()
    own_block = (own_qk_ref[...], own_value_ref[...])
    own_row = bucket_ref[pl.ds(own, 1), :].astype(jnp.float32)
    extend(own_block, own_row, query_ref, key_ref, value_ref, slice(0, tok_rows), bucket_count)
    for block, score_ref in enumerate(score_refs):
        start = block * query_rows
        score_ref[:, early] = products(query_ref[start : start + query_rows, :], key_ref[early, :])
        replace_diagonal(score_ref, start, tok_rows, head_dim)


def attend_early(bucket_heads, shared_qk, values, blocks, bucket_count):
    source_count, tok_rows = bucket_heads.shape
    head_dim = shared_qk.shape[1] // source_count
    rows = source_count * tok_rows
    own = pltpu.VMEM((tok_rows, head_dim), shared_qk.dtype)
    return pl.pallas_call(
        functools.partial(early_kernel, bucket_count=bucket_count),
        in_specs=in_hbm(3) + in_vmem(len(blocks)),
        out_specs=in_vmem(5),
        out_shape=[pltpu.VMEM((rows, 2 * head_dim), shared_qk.dtype)] * 3
        + [pltpu.VMEM((2 * tok_rows, rows), jnp.float32)] * 2,
        scratch_shapes=[
            pltpu.VMEM(bucket_heads.shape, bucket_heads.dtype),
            *(own, own),
            pltpu.SemaphoreType.DMA((3,)),
        ],
        compiler_params=vmem_params(8),
        name="attend_early",
    )(*(stays_in_hbm(array) for array in (bucket_heads, shared_qk, values)), *blocks)


def attend_kernel(*refs, bucket_count):
    refs, (late_score_ref, first_term_ref, second_term_ref) = refs[:-3], refs[-3:]
    query_rows, token_count = first_term_ref.shape
    tok_rows = query_rows // 2
    source_count = token_count // tok_rows
    pair_count = source_count // 2
    refs, (query_ref, key_ref, value_ref, *score_refs) = refs[:-5], refs[-5:]
    score_refs.append(late_score_ref)
    block_refs, out_refs = refs[5:-pair_count], refs[-pair_count:]
    head_dim = out_refs[0].shape[2]
    own = lax.axis_index("seq")
    owners = [(-step % pair_count, (own + flip) % 2) for step, flip in ((0, 0), *moves(source_count))]
    scale = 1.0 / math.sqrt(head_dim)
    strip = 16
    blocks = token_count // query_rows
    ahead = 2

    def scores_of(block, keys):
        queries = query_ref[block * query_rows : (block + 1) * query_rows, :]
        score_refs[block % 3][:, keys] = products(queries, key_ref[keys, :])

    def terms_of(score_ref, term_ref):
        for at in range(0, query_rows, strip):
            scores = score_ref[at : at + strip, :]
            row_max = jnp.max(scores, axis=1, keepdims=True)
            terms = jnp.exp2((scores - row_max) * (scale * math.log2(math.e)))
            term_ref[at : at + strip, :] = terms.astype(term_ref.dtype)

    def attend_of(block, term_ref):
        both = jnp.dot(term_ref[...], value_ref[...], preferred_element_type=jnp.float32)
        attended = (both[:, :head_dim] / both[:, head_dim:]).astype(out_refs[0].dtype)
        for at in range(0, query_rows, tok_rows):
            step, which = owners[(block * query_rows + at) // tok_rows]
            out_refs[step][which] = attended[at : at + tok_rows]

    for at, block_ref in enumerate(block_refs):
        stop = (source_count - len(block_refs) + at + 1) * tok_rows
        extend_received(block_ref, query_ref, key_ref, value_ref, slice(stop - tok_rows, stop), bucket_count)
        if stop % query_rows == 0:
            for block in range(ahead):
                scores_of(block, slice(stop - query_rows, stop))
    for block in range(blocks):
        if block + ahead < blocks:
            scores_of(block + ahead, slice(0, token_count))
            replace_diagonal(score_refs[(block + ahead) % 3], (block + ahead) * query_rows, tok_rows, head_dim)
        term_ref = (first_term_ref, second_term_ref)[block % 2]
        terms_of(score_refs[block % 3], term_ref)
        attend_of(block, term_ref)


def attend_head(early, blocks, bucket_count):
    token_count, head_dim = early[0].shape[0], early[0].shape[1] // 2
    tok_rows = early[-1].shape[0] // 2
    pair_count = token_count // (2 * tok_rows)
    dtype = early[0].dtype
    terms = pltpu.VMEM((2 * tok_rows, token_count), dtype)
    outs = pl.pallas_call(
        functools.partial(attend_kernel, bucket_count=bucket_count),
        in_specs=in_vmem(len(early) + len(blocks)),
        out_specs=in_vmem(pair_count + len(early)),
        out_shape=[pltpu.VMEM((2, tok_rows, head_dim), dtype)] * pair_count
        + [pltpu.VMEM(array.shape, array.dtype) for array in early],
        input_output_aliases={at: pair_count + at for at in range(len(early))},
        scratch_shapes=[pltpu.VMEM(early[-1].shape, early[-1].dtype), terms, terms],
        compiler_params=vmem_params(20),
        name="attend_head",
    )(*early, *blocks)
    return outs[:pair_count]


def fetch_kernel(w_hbm, after_ref, w_ref, sems):
    width = w_ref.shape[1]
    theirs = pl.multiple_of((1 - lax.axis_index("mp")) * width, width)
    rows = w_ref.shape[0] // FETCHES
    pieces = [slice(at * rows, (at + 1) * rows) for at in range(FETCHES)]
    fetches = [
        pltpu.make_async_copy(w_hbm.at[piece, pl.ds(theirs, width)], w_ref.at[piece, :], sems.at[at])
        for at, piece in enumerate(pieces)
    ]
    for fetch in fetches:
        fetch.start()
    for fetch in fetches:
        fetch.wait()


def fetch_theirs(w_out, after):
    return pl.pallas_call(
        fetch_kernel,
        in_specs=in_hbm(1) + in_vmem(1),
        out_specs=in_vmem(1)[0],
        out_shape=pltpu.VMEM((w_out.shape[0], w_out.shape[1] // 2), w_out.dtype),
        scratch_shapes=[pltpu.SemaphoreType.DMA((FETCHES,))],
        compiler_params=vmem_params(8),
        name="fetch_theirs",
    )(stays_in_hbm(w_out), after)


def gather_kernel(*refs):
    other = 1 - lax.axis_index("seq") % 2
    for at, pair_ref in enumerate(refs[:-1]):
        refs[-1][at] = pair_ref[other]


def gather_other(pairs):
    _, tok_rows, head_dim = pairs[0].shape
    return pl.pallas_call(
        gather_kernel,
        in_specs=in_vmem(len(pairs)),
        out_specs=in_vmem(1)[0],
        out_shape=pltpu.VMEM((len(pairs), tok_rows, head_dim), pairs[0].dtype),
        compiler_params=vmem_params(8),
        name="gather_other",
    )(*pairs)


def widen_kernel(*refs, pair_count):
    refs, (w_ref, out_ref, wide_ref) = refs[:-3], refs[-3:]
    pair_refs, swapped_refs = refs[:pair_count], refs[pair_count:]
    _, _, head_dim = pair_refs[0].shape
    swapped = [ref.at[at] for ref in swapped_refs for at in range(ref.shape[0])]
    own = lax.axis_index("seq")
    for step, pair_ref in enumerate(pair_refs):
        pair = (own // 2 + pair_count - step) % pair_count
        for rows, which in ((pair_ref[own % 2], own % 2), (swapped[step][...], 1 - own % 2)):
            start = pl.multiple_of((pair * 2 + which) * head_dim, head_dim)
            wide_ref[:, pl.ds(start, head_dim)] = rows
    out_ref[...] = jnp.dot(
        wide_ref[...], w_ref[:, : out_ref.shape[1]], preferred_element_type=jnp.float32
    ).astype(out_ref.dtype)


def widen_and_project(pairs, swapped, w_theirs, columns):
    tok_rows = pairs[0].shape[1]
    return pl.pallas_call(
        functools.partial(widen_kernel, pair_count=len(pairs)),
        in_specs=in_vmem(len(pairs) + len(swapped) + 1),
        out_specs=in_vmem(2),
        out_shape=[
            pltpu.VMEM((tok_rows, columns), w_theirs.dtype),
            pltpu.VMEM((tok_rows, w_theirs.shape[0]), w_theirs.dtype),
        ],
        compiler_params=vmem_params(16),
        name="widen_and_project",
    )(*pairs, *swapped, w_theirs)


def theirs_kernel(wide_ref, w_ref, out_ref, *, start):
    out_ref[...] = jnp.dot(
        wide_ref[...], w_ref[:, start : start + out_ref.shape[1]], preferred_element_type=jnp.float32
    ).astype(out_ref.dtype)


def project_theirs(wide, w_theirs, start):
    return pl.pallas_call(
        functools.partial(theirs_kernel, start=start),
        in_specs=in_vmem(2),
        out_specs=in_vmem(1)[0],
        out_shape=pltpu.VMEM((wide.shape[0], w_theirs.shape[1] - start), wide.dtype),
        compiler_params=vmem_params(16),
        name="project_theirs",
    )(wide, w_theirs)


def ours_kernel(wide_ref, w_hbm, out_ref, w_ref, sems):
    chunks, _, columns = w_ref.shape
    start = pl.multiple_of(lax.axis_index("mp") * (chunks * columns), columns)
    copies = [
        pltpu.make_async_copy(w_hbm.at[:, pl.ds(start + chunk * columns, columns)], w_ref.at[chunk], sems.at[chunk])
        for chunk in range(chunks)
    ]
    for copy in copies:
        copy.start()
    for chunk, copy in enumerate(copies):
        copy.wait()
        out_ref[:, chunk * columns : (chunk + 1) * columns] = jnp.dot(
            wide_ref[...], w_ref[chunk], preferred_element_type=jnp.float32
        )


def project_ours(wide, w_out):
    tok_rows, depth = wide.shape
    chunks = 4
    columns = w_out.shape[1] // (2 * chunks)
    return pl.pallas_call(
        ours_kernel,
        in_specs=in_vmem(1) + in_hbm(1),
        out_specs=in_vmem(1)[0],
        out_shape=pltpu.VMEM((tok_rows, chunks * columns), jnp.float32),
        scratch_shapes=[
            pltpu.VMEM((chunks, depth, columns), w_out.dtype),
            pltpu.SemaphoreType.DMA((chunks,)),
        ],
        compiler_params=vmem_params(20),
        name="project_ours",
    )(wide, stays_in_hbm(w_out))


def add_kernel(ours_ref, *refs):
    out_ref = refs[-1]
    start = 0
    for theirs_ref in refs[:-1]:
        at = slice(start, start + theirs_ref.shape[1])
        start = at.stop
        out_ref[:, at] = (ours_ref[:, at] + theirs_ref[...].astype(jnp.float32)).astype(out_ref.dtype)


def add_parts(ours, theirs, dtype):
    return pl.pallas_call(
        add_kernel,
        in_specs=in_vmem(1 + len(theirs)),
        out_shape=jax.ShapeDtypeStruct(ours.shape, dtype),
        compiler_params=vmem_params(8),
        name="add_parts",
    )(ours, *theirs)


def local_by_head(shared_qk, values, buckets, counts, w_out):
    bucket_heads = buckets.T
    seq_count = lax.axis_size("seq")
    received = [
        sent(block, step, flip)
        for (step, flip), block in zip(moves(seq_count), pack_blocks(bucket_heads, shared_qk, values))
    ]
    bucket_count = counts.shape[2]
    first_count = 2 * (5 * seq_count // 16) - 1
    early = attend_early(bucket_heads, shared_qk, values, received[:first_count], bucket_count)
    pairs = list(attend_head(early, received[first_count:], bucket_count))
    w_theirs = fetch_theirs(w_out, pairs[0])
    *others, last = pairs[1:]
    pairs = pairs[:1] + [sent(pair, step + 1, 0) for step, pair in enumerate(others)]
    pairs.append(sent(last, len(pairs), 0))
    cut = len(pairs) // 2 + 1
    swapped = [sent(gather_other(some), 0, 1) for some in (pairs[:cut], pairs[cut:])]
    columns = w_theirs.shape[1] // 4
    first, wide = widen_and_project(pairs, swapped, w_theirs, columns)
    peers = [(0, 1), (1, 0)]
    arrived = [lax.ppermute(first, "mp", peers)]
    rest = project_theirs(wide, w_theirs, columns)
    arrived.append(lax.ppermute(rest, "mp", peers))
    ours = project_ours(wide, w_out)
    return add_parts(ours, arrived, shared_qk.dtype)


def local(shared_qk, values, buckets, counts, w_out):
    head_count = buckets.shape[1]
    seq_count = lax.axis_size("seq")
    one_head_each = head_count == seq_count and counts.shape[2] == seq_count and 8 <= seq_count <= 128 and seq_count % 2 == 0
    if one_head_each and lax.axis_size("mp") == 2 and 2 * shared_qk.shape[0] <= BLOCK:
        return local_by_head(shared_qk, values, buckets, counts, w_out)
    return local_by_bucket(shared_qk, values, buckets, counts, w_out)


def solution(mesh):
    placed = (P("seq", "mp"), P("seq", "mp"), P("seq", "mp"), P(None, "mp", None), P("mp", None))
    return jax.shard_map(
        local, mesh=mesh, in_specs=placed, out_specs=P("seq", "mp"), check_vma=False
    )
```

```python
import functools
import math

import jax
import jax.numpy as jnp
from jax import lax
from jax.experimental import pallas as pl
from jax.experimental.pallas import tpu as pltpu
from jax.sharding import PartitionSpec as P


BLOCK = 256
MASKED = -1e30


SELF_SCORE = -100000.0


def passed_along(shard, axis, by):
    devices = lax.axis_size(axis)
    return lax.ppermute(shard, axis, [(i, (i + by) % devices) for i in range(devices)])


def block_attention(queries, window, window_live):
    head_dim = queries.shape[-1]
    block_rows = queries.shape[-2]
    key_rows = window[..., :head_dim]
    value_rows = window[..., head_dim:]
    scores = jnp.einsum("cqd,ckd->cqk", queries, key_rows, preferred_element_type=jnp.float32) * (
        1.0 / math.sqrt(head_dim)
    )
    query_place = jnp.arange(block_rows)[:, None] + block_rows
    key_place = jnp.arange(2 * block_rows)[None, :]
    itself = query_place == key_place
    scores = jnp.where(itself[None], SELF_SCORE, scores)
    allowed = window_live[:, None, :] | itself[None]
    row_max = jnp.max(jnp.where(allowed, scores, -1e30), axis=-1, keepdims=True)
    exp_terms = jnp.where(allowed, jnp.exp(scores - row_max), 0.0)
    weights = (exp_terms / jnp.sum(exp_terms, axis=-1, keepdims=True)).astype(jnp.bfloat16)
    attended = jnp.einsum("cqk,ckd->cqd", weights, value_rows, preferred_element_type=jnp.float32)
    return attended.astype(jnp.bfloat16)


def owner_layout(received, column, slot_count):
    source_count = column.shape[0]
    head_count = column.shape[1]
    upto_count = jnp.cumsum(column, axis=0)
    before_count = upto_count - column
    bucket_total = upto_count[-1]
    slot_range = jnp.arange(slot_count)
    source_dev = jnp.sum(upto_count[:, :, None] <= slot_range[None, None, :], axis=0)
    source_dev = jnp.minimum(source_dev, source_count - 1)
    source_range = jnp.arange(source_count)
    source_start = jnp.sum(
        jnp.where(source_dev[None] == source_range[:, None, None], before_count[:, :, None], 0),
        axis=0,
    )
    entry_row = jnp.clip(slot_range[None, :] - source_start, 0, received.shape[2] - 1)
    head_range = jnp.arange(head_count)
    layout = received[source_dev, head_range[:, None], entry_row]
    live = slot_range[None, :] < bucket_total[:, None]
    layout = jnp.where(live[..., None], layout, jnp.zeros((), layout.dtype))
    return (layout, live, before_count, bucket_total)


def tail_live(bucket_total, block_rows):
    return bucket_total[:, None] - block_rows + jnp.arange(block_rows)[None, :] >= 0


def last_rows(layout, bucket_total, block_rows):
    rank_index = bucket_total[:, None] - block_rows + jnp.arange(block_rows)[None, :]
    head_range = jnp.arange(layout.shape[0])
    rows = layout[head_range[:, None], jnp.maximum(rank_index, 0)]
    return jnp.where((rank_index >= 0)[..., None], rows, jnp.zeros((), rows.dtype))


def local_by_bucket(shared_qk, values, buckets, counts, w_out):
    tok_rows = shared_qk.shape[0]
    head_count = buckets.shape[1]
    head_dim = shared_qk.shape[1] // head_count
    seq_count = lax.axis_size("seq")
    capacity = 2 * tok_rows // seq_count
    slot_count = seq_count * capacity
    block_rows = BLOCK
    block_count = slot_count // block_rows
    own_index = lax.axis_index("seq")
    prev_index = (own_index + seq_count - 1) % seq_count
    head_range = jnp.arange(head_count)
    bucket_heads = buckets.T
    positions = jnp.arange(tok_rows)
    earlier = positions[None, :] < positions[:, None]
    same_bucket = bucket_heads[:, :, None] == bucket_heads[:, None, :]
    within = jnp.sum(same_bucket & earlier[None], axis=2)
    own_counts = lax.dynamic_index_in_dim(counts, own_index, 0, keepdims=False)
    own_starts = jnp.cumsum(own_counts, axis=1) - own_counts
    bucket_range = jnp.arange(seq_count)
    one_hot = bucket_heads[:, :, None] == bucket_range[None, None, :]
    token_start = jnp.sum(jnp.where(one_hot, own_starts[:, None, :], 0), axis=2)
    sorted_pos = token_start + within
    token_order = jnp.sum(
        jnp.where(sorted_pos[:, :, None] == positions[None, None, :], positions[None, :, None], 0),
        axis=1,
    )
    slot_range = jnp.arange(capacity)
    send_index = own_starts.T[:, :, None] + slot_range[None, None, :]
    filled = slot_range[None, None, :] < own_counts.T[:, :, None]
    token_pick = token_order[head_range[None, :, None], jnp.minimum(send_index, tok_rows - 1)]
    packed = jnp.concatenate(
        [
            shared_qk.reshape(tok_rows, head_count, head_dim),
            values.reshape(tok_rows, head_count, head_dim),
        ],
        axis=2,
    )
    outgoing = packed[token_pick, head_range[None, :, None]]
    outgoing = jnp.where(filled[..., None], outgoing, jnp.zeros((), outgoing.dtype))
    own_column = lax.dynamic_index_in_dim(counts, own_index, 2, keepdims=False)
    prev_column = lax.dynamic_index_in_dim(counts, prev_index, 2, keepdims=False)
    prev_total = jnp.sum(prev_column, axis=0)
    received = lax.all_to_all(outgoing, "seq", split_axis=0, concat_axis=0, tiled=True)
    layout, live, before_count, bucket_total = owner_layout(received, own_column, slot_count)
    tail_rows = last_rows(layout, bucket_total, block_rows)
    prev_rows = passed_along(tail_rows, "seq", 1)
    prev_live = tail_live(prev_total, block_rows)
    keys_all = jnp.concatenate([prev_rows, layout], axis=1)
    live_all = jnp.concatenate([prev_live, live], axis=1)
    window = jnp.concatenate(
        [
            keys_all[:, :slot_count].reshape(head_count, block_count, block_rows, 2 * head_dim),
            keys_all[:, block_rows:].reshape(head_count, block_count, block_rows, 2 * head_dim),
        ],
        axis=2,
    )
    window_live = jnp.concatenate(
        [
            live_all[:, :slot_count].reshape(head_count, block_count, block_rows),
            live_all[:, block_rows:].reshape(head_count, block_count, block_rows),
        ],
        axis=2,
    )
    queries = layout[..., :head_dim].reshape(head_count, block_count, block_rows, head_dim)
    attended = lax.map(
        lambda per_head: block_attention(per_head[0], per_head[1], per_head[2]),
        (queries, window, window_live),
    )
    out_layout = attended.reshape(head_count, slot_count, head_dim)
    back_index = before_count[:, :, None] + slot_range[None, None, :]
    back_filled = slot_range[None, None, :] < own_column[:, :, None]
    back_rows = out_layout[head_range[None, :, None], jnp.minimum(back_index, slot_count - 1)]
    back_rows = jnp.where(back_filled[..., None], back_rows, jnp.zeros((), back_rows.dtype))
    returned = lax.all_to_all(back_rows, "seq", split_axis=0, concat_axis=0, tiled=True)
    token_out = returned[buckets, head_range[None, :], within.T]
    token_out = token_out.reshape(tok_rows, head_count * head_dim)
    partial_sum = jnp.dot(token_out, w_out, preferred_element_type=jnp.float32)
    projected = lax.psum_scatter(partial_sum, "mp", scatter_dimension=1, tiled=True)
    return projected.astype(jnp.bfloat16)


PAD_ROWS = 8
FETCHES = 8
ADD_PIECES = 4


def in_vmem(count):
    return [pl.BlockSpec(memory_space=pltpu.VMEM)] * count


def in_hbm(count):
    return [pl.BlockSpec(memory_space=pltpu.HBM)] * count


def stays_in_hbm(array):
    return pltpu.with_memory_space_constraint(array, pltpu.HBM)


def vmem_params(mebibytes):
    return pltpu.CompilerParams(vmem_limit_bytes=mebibytes * 2**20)


def moves(count):
    every = [(step, flip) for step in range(count // 2) for flip in range(2)]
    return sorted(every[1:], key=lambda move: (move[0] % 2, move[1], move[0]))


def moved(index, step, flip, count):
    return (index // 2 + step) % (count // 2) * 2 + (index % 2 + flip) % 2


def sent(block, step, flip):
    count = lax.axis_size("seq")
    return lax.ppermute(block, "seq", [(i, moved(i, step, flip, count)) for i in range(count)])


def block_copies(qk_hbm, value_hbm, head, qk_ref, value_ref, sems):
    head_dim = qk_ref.shape[1]
    columns = pl.ds(pl.multiple_of(head * head_dim, head_dim), head_dim)
    return [
        pltpu.make_async_copy(qk_hbm.at[:, columns], qk_ref, sems.at[0]),
        pltpu.make_async_copy(value_hbm.at[:, columns], value_ref, sems.at[1]),
    ]


def pack_kernel(bucket_hbm, qk_hbm, value_hbm, *refs):
    outs, (bucket_ref, bucket_sem, sems) = refs[:-3], refs[-3:]
    head_count = bucket_ref.shape[0]
    tok_rows = qk_hbm.shape[0]
    own = lax.axis_index("seq")
    heads = [moved(own, step, flip, head_count) for step, flip in moves(head_count)]
    fetch_buckets = pltpu.make_async_copy(bucket_hbm, bucket_ref, bucket_sem)
    fetch_buckets.start()
    copies = []
    for at, (head, out) in enumerate(zip(heads, outs)):
        qk_ref, value_ref = out.at[:tok_rows, :], out.at[tok_rows : 2 * tok_rows, :]
        copies += block_copies(qk_hbm, value_hbm, head, qk_ref, value_ref, sems.at[at])
    for copy in copies:
        copy.start()
    fetch_buckets.wait()
    for head, out in zip(heads, outs):
        bucket = bucket_ref[pl.ds(head, 1), :].astype(jnp.float32)
        out[2 * tok_rows :, :] = jnp.broadcast_to(bucket, (PAD_ROWS, tok_rows)).astype(out.dtype)
    for copy in copies:
        copy.wait()


def pack_blocks(bucket_heads, shared_qk, values):
    head_count, tok_rows = bucket_heads.shape
    head_dim = shared_qk.shape[1] // head_count
    block = pltpu.VMEM((2 * tok_rows + PAD_ROWS, head_dim), shared_qk.dtype)
    return pl.pallas_call(
        pack_kernel,
        in_specs=in_hbm(3),
        out_specs=in_vmem(head_count - 1),
        out_shape=[block] * (head_count - 1),
        scratch_shapes=[
            pltpu.VMEM(bucket_heads.shape, bucket_heads.dtype),
            pltpu.SemaphoreType.DMA(()),
            pltpu.SemaphoreType.DMA((head_count - 1, 2)),
        ],
        compiler_params=vmem_params(8),
        name="pack_blocks",
    )(*(stays_in_hbm(array) for array in (bucket_heads, shared_qk, values)))


def extend(block, bucket_row, query_ref, key_ref, value_ref, rows, bucket_count):
    qk, value = block
    tok_rows, head_dim = value.shape
    lane = lax.broadcasted_iota(jnp.int32, (tok_rows, head_dim), 1)
    query_ref[rows, :head_dim] = qk
    key_ref[rows, :head_dim] = qk
    value_ref[rows, :head_dim] = value
    value_ref[rows, head_dim:] = jnp.ones((tok_rows, head_dim), value_ref.dtype)
    bucket = jnp.broadcast_to(bucket_row, (head_dim, tok_rows)).T.astype(jnp.int32)
    following = jnp.where(bucket == bucket_count - 1, 0, bucket + 1)
    same = lane == bucket
    query_ref[rows, head_dim:] = jnp.where(same, 1.0, 0.0).astype(query_ref.dtype)
    key_ref[rows, head_dim:] = jnp.where(same | (lane == following), 0.0, MASKED).astype(key_ref.dtype)


def extend_received(block_ref, query_ref, key_ref, value_ref, rows, bucket_count):
    tok_rows = (block_ref.shape[0] - PAD_ROWS) // 2
    block = (block_ref[:tok_rows, :], block_ref[tok_rows : 2 * tok_rows, :])
    bucket_row = block_ref[2 * tok_rows :, :].astype(jnp.float32)[:1]
    extend(block, bucket_row, query_ref, key_ref, value_ref, rows, bucket_count)


def products(queries, keys):
    return lax.dot_general(queries, keys, (((1,), (1,)), ((), ())), preferred_element_type=jnp.float32)


def replace_diagonal(score_ref, start, size, head_dim):
    square = (size, size)
    itself = lax.broadcasted_iota(jnp.int32, square, 0) == lax.broadcasted_iota(jnp.int32, square, 1)
    replaced = SELF_SCORE * math.sqrt(head_dim)
    for at in range(0, score_ref.shape[0], size):
        columns = slice(start + at, start + at + size)
        diagonal = score_ref[at : at + size, columns]
        score_ref[at : at + size, columns] = jnp.where(itself, replaced, diagonal)


def fetches_of(w_hbm, w_ref, start, sems):
    width = w_hbm.shape[1] // 2
    theirs = (1 - lax.axis_index("mp")) * width + start
    columns = pl.ds(pl.multiple_of(theirs, math.gcd(width, start)), w_ref.shape[1])
    rows = w_ref.shape[0] // FETCHES
    pieces = [slice(at * rows, (at + 1) * rows) for at in range(FETCHES)]
    return [
        pltpu.make_async_copy(w_hbm.at[piece, columns], w_ref.at[piece, :], sems.at[at])
        for at, piece in enumerate(pieces)
    ]


def early_kernel(bucket_hbm, qk_hbm, value_hbm, w_hbm, *refs, bucket_count):
    refs, (bucket_ref, own_qk_ref, own_value_ref, sems, fetch_sems) = refs[:-5], refs[-5:]
    block_refs, (w_ref, query_ref, key_ref, value_ref, *score_refs) = refs[:-6], refs[-6:]
    tok_rows, head_dim = own_qk_ref.shape
    query_rows = score_refs[0].shape[0]
    own = lax.axis_index("seq")
    copies = block_copies(qk_hbm, value_hbm, own, own_qk_ref, own_value_ref, sems)
    copies.append(pltpu.make_async_copy(bucket_hbm, bucket_ref, sems.at[2]))
    fetches = fetches_of(w_hbm, w_ref, 0, fetch_sems)
    for copy in (*copies, *fetches):
        copy.start()
    for at, block_ref in enumerate(block_refs):
        rows = slice((at + 1) * tok_rows, (at + 2) * tok_rows)
        extend_received(block_ref, query_ref, key_ref, value_ref, rows, bucket_count)
    early = slice(0, (len(block_refs) + 1) * tok_rows)
    for copy in copies:
        copy.wait()
    own_block = (own_qk_ref[...], own_value_ref[...])
    own_row = bucket_ref[pl.ds(own, 1), :].astype(jnp.float32)
    extend(own_block, own_row, query_ref, key_ref, value_ref, slice(0, tok_rows), bucket_count)
    for block, score_ref in enumerate(score_refs):
        start = block * query_rows
        score_ref[:, early] = products(query_ref[start : start + query_rows, :], key_ref[early, :])
        replace_diagonal(score_ref, start, tok_rows, head_dim)
    for fetch in fetches:
        fetch.wait()


def attend_early(bucket_heads, shared_qk, values, w_out, blocks, bucket_count):
    source_count, tok_rows = bucket_heads.shape
    head_dim = shared_qk.shape[1] // source_count
    rows = source_count * tok_rows
    own = pltpu.VMEM((tok_rows, head_dim), shared_qk.dtype)
    return pl.pallas_call(
        functools.partial(early_kernel, bucket_count=bucket_count),
        in_specs=in_hbm(4) + in_vmem(len(blocks)),
        out_specs=in_vmem(6),
        out_shape=[pltpu.VMEM((w_out.shape[0], w_out.shape[1] // 8), w_out.dtype)]
        + [pltpu.VMEM((rows, 2 * head_dim), shared_qk.dtype)] * 3
        + [pltpu.VMEM((2 * tok_rows, rows), jnp.float32)] * 2,
        scratch_shapes=[
            pltpu.VMEM(bucket_heads.shape, bucket_heads.dtype),
            *(own, own),
            pltpu.SemaphoreType.DMA((3,)),
            pltpu.SemaphoreType.DMA((FETCHES,)),
        ],
        compiler_params=vmem_params(12),
        name="attend_early",
    )(*(stays_in_hbm(array) for array in (bucket_heads, shared_qk, values, w_out)), *blocks)


def attend_kernel(*refs, bucket_count):
    refs, (late_score_ref, first_term_ref, second_term_ref) = refs[:-3], refs[-3:]
    query_rows, token_count = first_term_ref.shape
    tok_rows = query_rows // 2
    source_count = token_count // tok_rows
    pair_count = source_count // 2
    refs, (query_ref, key_ref, value_ref, *score_refs) = refs[:-5], refs[-5:]
    score_refs.append(late_score_ref)
    block_refs, out_refs = refs[5:-pair_count], refs[-pair_count:]
    head_dim = out_refs[0].shape[2]
    own = lax.axis_index("seq")
    owners = [(-step % pair_count, (own + flip) % 2) for step, flip in ((0, 0), *moves(source_count))]
    scale = 1.0 / math.sqrt(head_dim)
    strip = 16
    blocks = token_count // query_rows
    ahead = 2

    def scores_of(block, keys):
        queries = query_ref[block * query_rows : (block + 1) * query_rows, :]
        score_refs[block % 3][:, keys] = products(queries, key_ref[keys, :])

    def terms_of(score_ref, term_ref):
        for at in range(0, query_rows, strip):
            scores = score_ref[at : at + strip, :]
            row_max = jnp.max(scores, axis=1, keepdims=True)
            terms = jnp.exp2((scores - row_max) * (scale * math.log2(math.e)))
            term_ref[at : at + strip, :] = terms.astype(term_ref.dtype)

    def attend_of(block, term_ref):
        both = jnp.dot(term_ref[...], value_ref[...], preferred_element_type=jnp.float32)
        attended = (both[:, :head_dim] / both[:, head_dim:]).astype(out_refs[0].dtype)
        for at in range(0, query_rows, tok_rows):
            step, which = owners[(block * query_rows + at) // tok_rows]
            out_refs[step][which] = attended[at : at + tok_rows]

    for at, block_ref in enumerate(block_refs):
        stop = (source_count - len(block_refs) + at + 1) * tok_rows
        extend_received(block_ref, query_ref, key_ref, value_ref, slice(stop - tok_rows, stop), bucket_count)
        if stop % query_rows == 0:
            for block in range(ahead):
                scores_of(block, slice(stop - query_rows, stop))
    for block in range(blocks):
        if block + ahead < blocks:
            scores_of(block + ahead, slice(0, token_count))
            replace_diagonal(score_refs[(block + ahead) % 3], (block + ahead) * query_rows, tok_rows, head_dim)
        term_ref = (first_term_ref, second_term_ref)[block % 2]
        terms_of(score_refs[block % 3], term_ref)
        attend_of(block, term_ref)


def attend_head(early, blocks, bucket_count):
    token_count, head_dim = early[0].shape[0], early[0].shape[1] // 2
    tok_rows = early[-1].shape[0] // 2
    pair_count = token_count // (2 * tok_rows)
    dtype = early[0].dtype
    terms = pltpu.VMEM((2 * tok_rows, token_count), dtype)
    outs = pl.pallas_call(
        functools.partial(attend_kernel, bucket_count=bucket_count),
        in_specs=in_vmem(len(early) + len(blocks)),
        out_specs=in_vmem(pair_count + len(early)),
        out_shape=[pltpu.VMEM((2, tok_rows, head_dim), dtype)] * pair_count
        + [pltpu.VMEM(array.shape, array.dtype) for array in early],
        input_output_aliases={at: pair_count + at for at in range(len(early))},
        scratch_shapes=[pltpu.VMEM(early[-1].shape, early[-1].dtype), terms, terms],
        compiler_params=vmem_params(20),
        name="attend_head",
    )(*early, *blocks)
    return outs[:pair_count]


def fetch_kernel(w_hbm, after_ref, w_ref, sems):
    fetches = fetches_of(w_hbm, w_ref, w_hbm.shape[1] // 2 - w_ref.shape[1], sems)
    for fetch in fetches:
        fetch.start()
    for fetch in fetches:
        fetch.wait()


def fetch_theirs(w_out, after):
    return pl.pallas_call(
        fetch_kernel,
        in_specs=in_hbm(1) + in_vmem(1),
        out_specs=in_vmem(1)[0],
        out_shape=pltpu.VMEM((w_out.shape[0], w_out.shape[1] // 8 * 3), w_out.dtype),
        scratch_shapes=[pltpu.SemaphoreType.DMA((FETCHES,))],
        compiler_params=vmem_params(8),
        name="fetch_theirs",
    )(stays_in_hbm(w_out), after)


def gather_kernel(*refs):
    other = 1 - lax.axis_index("seq") % 2
    for at, pair_ref in enumerate(refs[:-1]):
        refs[-1][at] = pair_ref[other]


def gather_other(pairs):
    _, tok_rows, head_dim = pairs[0].shape
    return pl.pallas_call(
        gather_kernel,
        in_specs=in_vmem(len(pairs)),
        out_specs=in_vmem(1)[0],
        out_shape=pltpu.VMEM((len(pairs), tok_rows, head_dim), pairs[0].dtype),
        compiler_params=vmem_params(8),
        name="gather_other",
    )(*pairs)


def widen_kernel(*refs, pair_count):
    refs, (w_ref, out_ref, wide_ref) = refs[:-3], refs[-3:]
    pair_refs, swapped_refs = refs[:pair_count], refs[pair_count:]
    _, _, head_dim = pair_refs[0].shape
    swapped = [ref.at[at] for ref in swapped_refs for at in range(ref.shape[0])]
    own = lax.axis_index("seq")
    for step, pair_ref in enumerate(pair_refs):
        pair = (own // 2 + pair_count - step) % pair_count
        for rows, which in ((pair_ref[own % 2], own % 2), (swapped[step][...], 1 - own % 2)):
            start = pl.multiple_of((pair * 2 + which) * head_dim, head_dim)
            wide_ref[:, pl.ds(start, head_dim)] = rows
    out_ref[...] = jnp.dot(
        wide_ref[...], w_ref[:, : out_ref.shape[1]], preferred_element_type=jnp.float32
    ).astype(out_ref.dtype)


def widen_and_project(pairs, swapped, w_theirs, columns):
    tok_rows = pairs[0].shape[1]
    return pl.pallas_call(
        functools.partial(widen_kernel, pair_count=len(pairs)),
        in_specs=in_vmem(len(pairs) + len(swapped) + 1),
        out_specs=in_vmem(2),
        out_shape=[
            pltpu.VMEM((tok_rows, columns), w_theirs.dtype),
            pltpu.VMEM((tok_rows, w_theirs.shape[0]), w_theirs.dtype),
        ],
        compiler_params=vmem_params(16),
        name="widen_and_project",
    )(*pairs, *swapped, w_theirs)


def theirs_kernel(wide_ref, w_ref, out_ref, *, start):
    out_ref[...] = jnp.dot(
        wide_ref[...], w_ref[:, start : start + out_ref.shape[1]], preferred_element_type=jnp.float32
    ).astype(out_ref.dtype)


def project_theirs(wide, w_theirs, start):
    return pl.pallas_call(
        functools.partial(theirs_kernel, start=start),
        in_specs=in_vmem(2),
        out_specs=in_vmem(1)[0],
        out_shape=pltpu.VMEM((wide.shape[0], w_theirs.shape[1] - start), wide.dtype),
        compiler_params=vmem_params(16),
        name="project_theirs",
    )(wide, w_theirs)


def ours_kernel(wide_ref, w_hbm, out_ref, w_ref, sems):
    chunks, _, columns = w_ref.shape
    start = pl.multiple_of(lax.axis_index("mp") * (chunks * columns), columns)
    copies = [
        pltpu.make_async_copy(w_hbm.at[:, pl.ds(start + chunk * columns, columns)], w_ref.at[chunk], sems.at[chunk])
        for chunk in range(chunks)
    ]
    for copy in copies:
        copy.start()
    for chunk, copy in enumerate(copies):
        copy.wait()
        out_ref[:, chunk * columns : (chunk + 1) * columns] = jnp.dot(
            wide_ref[...], w_ref[chunk], preferred_element_type=jnp.float32
        )


def project_ours(wide, w_out):
    tok_rows, depth = wide.shape
    chunks = 4
    columns = w_out.shape[1] // (2 * chunks)
    return pl.pallas_call(
        ours_kernel,
        in_specs=in_vmem(1) + in_hbm(1),
        out_specs=in_vmem(1)[0],
        out_shape=pltpu.VMEM((tok_rows, chunks * columns), jnp.float32),
        scratch_shapes=[
            pltpu.VMEM((chunks, depth, columns), w_out.dtype),
            pltpu.SemaphoreType.DMA((chunks,)),
        ],
        compiler_params=vmem_params(20),
        name="project_ours",
    )(wide, stays_in_hbm(w_out))


def add_kernel(ours_ref, *refs):
    theirs_refs, (out_hbm, sum_ref, sems) = refs[:-3], refs[-3:]
    width = ours_ref.shape[1] // ADD_PIECES
    copies = []
    for piece in range(ADD_PIECES):
        at = slice(piece * width, (piece + 1) * width)
        start = 0
        for theirs_ref in theirs_refs:
            stop = start + theirs_ref.shape[1]
            low, high = max(start, at.start), min(stop, at.stop)
            if low < high:
                theirs = theirs_ref[:, low - start : high - start].astype(jnp.float32)
                sum_ref[:, low:high] = (ours_ref[:, low:high] + theirs).astype(sum_ref.dtype)
            start = stop
        copies.append(pltpu.make_async_copy(sum_ref.at[:, at], out_hbm.at[:, at], sems.at[piece]))
        copies[-1].start()
    for copy in copies:
        copy.wait()


def add_parts(ours, theirs, dtype):
    return pl.pallas_call(
        add_kernel,
        in_specs=in_vmem(1 + len(theirs)),
        out_specs=in_hbm(1)[0],
        out_shape=jax.ShapeDtypeStruct(ours.shape, dtype),
        scratch_shapes=[pltpu.VMEM(ours.shape, dtype), pltpu.SemaphoreType.DMA((ADD_PIECES,))],
        compiler_params=vmem_params(8),
        name="add_parts",
    )(ours, *theirs)


def local_by_head(shared_qk, values, buckets, counts, w_out):
    bucket_heads = buckets.T
    seq_count = lax.axis_size("seq")
    received = [
        sent(block, step, flip)
        for (step, flip), block in zip(moves(seq_count), pack_blocks(bucket_heads, shared_qk, values))
    ]
    bucket_count = counts.shape[2]
    first_count = 2 * (5 * seq_count // 16) - 1
    w_first, *early = attend_early(bucket_heads, shared_qk, values, w_out, received[:first_count], bucket_count)
    pairs = list(attend_head(early, received[first_count:], bucket_count))
    w_rest = fetch_theirs(w_out, pairs[0])
    *others, last = pairs[1:]
    pairs = pairs[:1] + [sent(pair, step + 1, 0) for step, pair in enumerate(others)]
    pairs.append(sent(last, len(pairs), 0))
    cut = len(pairs) // 2 + 2
    swapped = [sent(gather_other(some), 0, 1) for some in (pairs[:cut], pairs[cut:])]
    first, wide = widen_and_project(pairs, swapped, w_first, w_first.shape[1])
    peers = [(0, 1), (1, 0)]
    arrived = [lax.ppermute(first, "mp", peers)]
    rest = project_theirs(wide, w_rest, 0)
    arrived.append(lax.ppermute(rest, "mp", peers))
    ours = project_ours(wide, w_out)
    return add_parts(ours, arrived, shared_qk.dtype)


def local(shared_qk, values, buckets, counts, w_out):
    head_count = buckets.shape[1]
    seq_count = lax.axis_size("seq")
    one_head_each = head_count == seq_count and counts.shape[2] == seq_count and 8 <= seq_count <= 128 and seq_count % 2 == 0
    if one_head_each and lax.axis_size("mp") == 2 and 2 * shared_qk.shape[0] <= BLOCK:
        return local_by_head(shared_qk, values, buckets, counts, w_out)
    return local_by_bucket(shared_qk, values, buckets, counts, w_out)


def solution(mesh):
    placed = (P("seq", "mp"), P("seq", "mp"), P("seq", "mp"), P(None, "mp", None), P("mp", None))
    return jax.shard_map(
        local, mesh=mesh, in_specs=placed, out_specs=P("seq", "mp"), check_vma=False
    )
```

```python
import functools
import math

import jax
import jax.numpy as jnp
from jax import lax
from jax.experimental import pallas as pl
from jax.experimental.pallas import tpu as pltpu
from jax.sharding import PartitionSpec as P


BLOCK = 256
MASKED = -1e30


SELF_SCORE = -100000.0


def passed_along(shard, axis, by):
    devices = lax.axis_size(axis)
    return lax.ppermute(shard, axis, [(i, (i + by) % devices) for i in range(devices)])


def block_attention(queries, window, window_live):
    head_dim = queries.shape[-1]
    block_rows = queries.shape[-2]
    key_rows = window[..., :head_dim]
    value_rows = window[..., head_dim:]
    scores = jnp.einsum("cqd,ckd->cqk", queries, key_rows, preferred_element_type=jnp.float32) * (
        1.0 / math.sqrt(head_dim)
    )
    query_place = jnp.arange(block_rows)[:, None] + block_rows
    key_place = jnp.arange(2 * block_rows)[None, :]
    itself = query_place == key_place
    scores = jnp.where(itself[None], SELF_SCORE, scores)
    allowed = window_live[:, None, :] | itself[None]
    row_max = jnp.max(jnp.where(allowed, scores, -1e30), axis=-1, keepdims=True)
    exp_terms = jnp.where(allowed, jnp.exp(scores - row_max), 0.0)
    weights = (exp_terms / jnp.sum(exp_terms, axis=-1, keepdims=True)).astype(jnp.bfloat16)
    attended = jnp.einsum("cqk,ckd->cqd", weights, value_rows, preferred_element_type=jnp.float32)
    return attended.astype(jnp.bfloat16)


def owner_layout(received, column, slot_count):
    source_count = column.shape[0]
    head_count = column.shape[1]
    upto_count = jnp.cumsum(column, axis=0)
    before_count = upto_count - column
    bucket_total = upto_count[-1]
    slot_range = jnp.arange(slot_count)
    source_dev = jnp.sum(upto_count[:, :, None] <= slot_range[None, None, :], axis=0)
    source_dev = jnp.minimum(source_dev, source_count - 1)
    source_range = jnp.arange(source_count)
    source_start = jnp.sum(
        jnp.where(source_dev[None] == source_range[:, None, None], before_count[:, :, None], 0),
        axis=0,
    )
    entry_row = jnp.clip(slot_range[None, :] - source_start, 0, received.shape[2] - 1)
    head_range = jnp.arange(head_count)
    layout = received[source_dev, head_range[:, None], entry_row]
    live = slot_range[None, :] < bucket_total[:, None]
    layout = jnp.where(live[..., None], layout, jnp.zeros((), layout.dtype))
    return (layout, live, before_count, bucket_total)


def tail_live(bucket_total, block_rows):
    return bucket_total[:, None] - block_rows + jnp.arange(block_rows)[None, :] >= 0


def last_rows(layout, bucket_total, block_rows):
    rank_index = bucket_total[:, None] - block_rows + jnp.arange(block_rows)[None, :]
    head_range = jnp.arange(layout.shape[0])
    rows = layout[head_range[:, None], jnp.maximum(rank_index, 0)]
    return jnp.where((rank_index >= 0)[..., None], rows, jnp.zeros((), rows.dtype))


def local_by_bucket(shared_qk, values, buckets, counts, w_out):
    tok_rows = shared_qk.shape[0]
    head_count = buckets.shape[1]
    head_dim = shared_qk.shape[1] // head_count
    seq_count = lax.axis_size("seq")
    capacity = 2 * tok_rows // seq_count
    slot_count = seq_count * capacity
    block_rows = BLOCK
    block_count = slot_count // block_rows
    own_index = lax.axis_index("seq")
    prev_index = (own_index + seq_count - 1) % seq_count
    head_range = jnp.arange(head_count)
    bucket_heads = buckets.T
    positions = jnp.arange(tok_rows)
    earlier = positions[None, :] < positions[:, None]
    same_bucket = bucket_heads[:, :, None] == bucket_heads[:, None, :]
    within = jnp.sum(same_bucket & earlier[None], axis=2)
    own_counts = lax.dynamic_index_in_dim(counts, own_index, 0, keepdims=False)
    own_starts = jnp.cumsum(own_counts, axis=1) - own_counts
    bucket_range = jnp.arange(seq_count)
    one_hot = bucket_heads[:, :, None] == bucket_range[None, None, :]
    token_start = jnp.sum(jnp.where(one_hot, own_starts[:, None, :], 0), axis=2)
    sorted_pos = token_start + within
    token_order = jnp.sum(
        jnp.where(sorted_pos[:, :, None] == positions[None, None, :], positions[None, :, None], 0),
        axis=1,
    )
    slot_range = jnp.arange(capacity)
    send_index = own_starts.T[:, :, None] + slot_range[None, None, :]
    filled = slot_range[None, None, :] < own_counts.T[:, :, None]
    token_pick = token_order[head_range[None, :, None], jnp.minimum(send_index, tok_rows - 1)]
    packed = jnp.concatenate(
        [
            shared_qk.reshape(tok_rows, head_count, head_dim),
            values.reshape(tok_rows, head_count, head_dim),
        ],
        axis=2,
    )
    outgoing = packed[token_pick, head_range[None, :, None]]
    outgoing = jnp.where(filled[..., None], outgoing, jnp.zeros((), outgoing.dtype))
    own_column = lax.dynamic_index_in_dim(counts, own_index, 2, keepdims=False)
    prev_column = lax.dynamic_index_in_dim(counts, prev_index, 2, keepdims=False)
    prev_total = jnp.sum(prev_column, axis=0)
    received = lax.all_to_all(outgoing, "seq", split_axis=0, concat_axis=0, tiled=True)
    layout, live, before_count, bucket_total = owner_layout(received, own_column, slot_count)
    tail_rows = last_rows(layout, bucket_total, block_rows)
    prev_rows = passed_along(tail_rows, "seq", 1)
    prev_live = tail_live(prev_total, block_rows)
    keys_all = jnp.concatenate([prev_rows, layout], axis=1)
    live_all = jnp.concatenate([prev_live, live], axis=1)
    window = jnp.concatenate(
        [
            keys_all[:, :slot_count].reshape(head_count, block_count, block_rows, 2 * head_dim),
            keys_all[:, block_rows:].reshape(head_count, block_count, block_rows, 2 * head_dim),
        ],
        axis=2,
    )
    window_live = jnp.concatenate(
        [
            live_all[:, :slot_count].reshape(head_count, block_count, block_rows),
            live_all[:, block_rows:].reshape(head_count, block_count, block_rows),
        ],
        axis=2,
    )
    queries = layout[..., :head_dim].reshape(head_count, block_count, block_rows, head_dim)
    attended = lax.map(
        lambda per_head: block_attention(per_head[0], per_head[1], per_head[2]),
        (queries, window, window_live),
    )
    out_layout = attended.reshape(head_count, slot_count, head_dim)
    back_index = before_count[:, :, None] + slot_range[None, None, :]
    back_filled = slot_range[None, None, :] < own_column[:, :, None]
    back_rows = out_layout[head_range[None, :, None], jnp.minimum(back_index, slot_count - 1)]
    back_rows = jnp.where(back_filled[..., None], back_rows, jnp.zeros((), back_rows.dtype))
    returned = lax.all_to_all(back_rows, "seq", split_axis=0, concat_axis=0, tiled=True)
    token_out = returned[buckets, head_range[None, :], within.T]
    token_out = token_out.reshape(tok_rows, head_count * head_dim)
    partial_sum = jnp.dot(token_out, w_out, preferred_element_type=jnp.float32)
    projected = lax.psum_scatter(partial_sum, "mp", scatter_dimension=1, tiled=True)
    return projected.astype(jnp.bfloat16)


PAD_ROWS = 8
FETCHES = 4


def in_vmem(count):
    return [pl.BlockSpec(memory_space=pltpu.VMEM)] * count


def in_hbm(count):
    return [pl.BlockSpec(memory_space=pltpu.HBM)] * count


def stays_in_hbm(array):
    return pltpu.with_memory_space_constraint(array, pltpu.HBM)


def vmem_params(mebibytes):
    return pltpu.CompilerParams(vmem_limit_bytes=mebibytes * 2**20)


def moves(count):
    every = [(step, flip) for step in range(count // 2) for flip in range(2)]
    return sorted(every[1:], key=lambda move: (move[0] % 2, move[1], move[0]))


def moved(index, step, flip, count):
    return (index // 2 + step) % (count // 2) * 2 + (index % 2 + flip) % 2


def sent(block, step, flip):
    count = lax.axis_size("seq")
    return lax.ppermute(block, "seq", [(i, moved(i, step, flip, count)) for i in range(count)])


def block_copies(qk_hbm, value_hbm, head, qk_ref, value_ref, sems):
    head_dim = qk_ref.shape[1]
    columns = pl.ds(pl.multiple_of(head * head_dim, head_dim), head_dim)
    return [
        pltpu.make_async_copy(qk_hbm.at[:, columns], qk_ref, sems.at[0]),
        pltpu.make_async_copy(value_hbm.at[:, columns], value_ref, sems.at[1]),
    ]


def pack_kernel(bucket_hbm, qk_hbm, value_hbm, *refs):
    outs, (bucket_ref, bucket_sem, sems) = refs[:-3], refs[-3:]
    head_count = bucket_ref.shape[0]
    tok_rows = qk_hbm.shape[0]
    own = lax.axis_index("seq")
    heads = [moved(own, step, flip, head_count) for step, flip in moves(head_count)]
    fetch_buckets = pltpu.make_async_copy(bucket_hbm, bucket_ref, bucket_sem)
    fetch_buckets.start()
    copies = []
    for at, (head, out) in enumerate(zip(heads, outs)):
        qk_ref, value_ref = out.at[:tok_rows, :], out.at[tok_rows : 2 * tok_rows, :]
        copies += block_copies(qk_hbm, value_hbm, head, qk_ref, value_ref, sems.at[at])
    for copy in copies:
        copy.start()
    fetch_buckets.wait()
    for head, out in zip(heads, outs):
        bucket = bucket_ref[pl.ds(head, 1), :].astype(jnp.float32)
        out[2 * tok_rows :, :] = jnp.broadcast_to(bucket, (PAD_ROWS, tok_rows)).astype(out.dtype)
    for copy in copies:
        copy.wait()


def pack_blocks(bucket_heads, shared_qk, values):
    head_count, tok_rows = bucket_heads.shape
    head_dim = shared_qk.shape[1] // head_count
    block = pltpu.VMEM((2 * tok_rows + PAD_ROWS, head_dim), shared_qk.dtype)
    return pl.pallas_call(
        pack_kernel,
        in_specs=in_hbm(3),
        out_specs=in_vmem(head_count - 1),
        out_shape=[block] * (head_count - 1),
        scratch_shapes=[
            pltpu.VMEM(bucket_heads.shape, bucket_heads.dtype),
            pltpu.SemaphoreType.DMA(()),
            pltpu.SemaphoreType.DMA((head_count - 1, 2)),
        ],
        compiler_params=vmem_params(8),
        name="pack_blocks",
    )(*(stays_in_hbm(array) for array in (bucket_heads, shared_qk, values)))


def extend(block, bucket_row, query_ref, key_ref, value_ref, rows, bucket_count):
    qk, value = block
    tok_rows, head_dim = value.shape
    lane = lax.broadcasted_iota(jnp.int32, (tok_rows, head_dim), 1)
    query_ref[rows, :head_dim] = qk
    key_ref[rows, :head_dim] = qk
    value_ref[rows, :head_dim] = value
    value_ref[rows, head_dim:] = jnp.ones((tok_rows, head_dim), value_ref.dtype)
    bucket = jnp.broadcast_to(bucket_row, (head_dim, tok_rows)).T.astype(jnp.int32)
    following = jnp.where(bucket == bucket_count - 1, 0, bucket + 1)
    same = lane == bucket
    query_ref[rows, head_dim:] = jnp.where(same, 1.0, 0.0).astype(query_ref.dtype)
    key_ref[rows, head_dim:] = jnp.where(same | (lane == following), 0.0, MASKED).astype(key_ref.dtype)


def extend_received(block_ref, query_ref, key_ref, value_ref, rows, bucket_count):
    tok_rows = (block_ref.shape[0] - PAD_ROWS) // 2
    block = (block_ref[:tok_rows, :], block_ref[tok_rows : 2 * tok_rows, :])
    bucket_row = block_ref[2 * tok_rows :, :].astype(jnp.float32)[:1]
    extend(block, bucket_row, query_ref, key_ref, value_ref, rows, bucket_count)


def products(queries, keys):
    return lax.dot_general(queries, keys, (((1,), (1,)), ((), ())), preferred_element_type=jnp.float32)


def replace_diagonal(score_ref, start, size, head_dim):
    square = (size, size)
    itself = lax.broadcasted_iota(jnp.int32, square, 0) == lax.broadcasted_iota(jnp.int32, square, 1)
    replaced = SELF_SCORE * math.sqrt(head_dim)
    for at in range(0, score_ref.shape[0], size):
        columns = slice(start + at, start + at + size)
        diagonal = score_ref[at : at + size, columns]
        score_ref[at : at + size, columns] = jnp.where(itself, replaced, diagonal)


def fetches_of(w_hbm, w_ref, start, sems):
    width = w_hbm.shape[1] // 2
    theirs = (1 - lax.axis_index("mp")) * width + start
    columns = pl.ds(pl.multiple_of(theirs, math.gcd(width, start)), w_ref.shape[1])
    rows = w_ref.shape[0] // FETCHES
    pieces = [slice(at * rows, (at + 1) * rows) for at in range(FETCHES)]
    return [
        pltpu.make_async_copy(w_hbm.at[piece, columns], w_ref.at[piece, :], sems.at[at])
        for at, piece in enumerate(pieces)
    ]


def early_kernel(bucket_hbm, qk_hbm, value_hbm, w_hbm, *refs, bucket_count):
    refs, (bucket_ref, own_qk_ref, own_value_ref, sems, fetch_sems) = refs[:-5], refs[-5:]
    block_refs, (w_ref, query_ref, key_ref, value_ref, *score_refs) = refs[:-6], refs[-6:]
    tok_rows, head_dim = own_qk_ref.shape
    query_rows = score_refs[0].shape[0]
    own = lax.axis_index("seq")
    copies = block_copies(qk_hbm, value_hbm, own, own_qk_ref, own_value_ref, sems)
    copies.append(pltpu.make_async_copy(bucket_hbm, bucket_ref, sems.at[2]))
    fetches = fetches_of(w_hbm, w_ref, 0, fetch_sems)
    for copy in (*copies, *fetches):
        copy.start()
    for at, block_ref in enumerate(block_refs):
        rows = slice((at + 1) * tok_rows, (at + 2) * tok_rows)
        extend_received(block_ref, query_ref, key_ref, value_ref, rows, bucket_count)
    early = slice(0, (len(block_refs) + 1) * tok_rows)
    for copy in copies:
        copy.wait()
    own_block = (own_qk_ref[...], own_value_ref[...])
    own_row = bucket_ref[pl.ds(own, 1), :].astype(jnp.float32)
    extend(own_block, own_row, query_ref, key_ref, value_ref, slice(0, tok_rows), bucket_count)
    for block, score_ref in enumerate(score_refs):
        start = block * query_rows
        score_ref[:, early] = products(query_ref[start : start + query_rows, :], key_ref[early, :])
        replace_diagonal(score_ref, start, tok_rows, head_dim)
    for fetch in fetches:
        fetch.wait()


def attend_early(bucket_heads, shared_qk, values, w_out, blocks, bucket_count):
    source_count, tok_rows = bucket_heads.shape
    head_dim = shared_qk.shape[1] // source_count
    rows = source_count * tok_rows
    own = pltpu.VMEM((tok_rows, head_dim), shared_qk.dtype)
    return pl.pallas_call(
        functools.partial(early_kernel, bucket_count=bucket_count),
        in_specs=in_hbm(4) + in_vmem(len(blocks)),
        out_specs=in_vmem(6),
        out_shape=[pltpu.VMEM((w_out.shape[0], w_out.shape[1] // 8), w_out.dtype)]
        + [pltpu.VMEM((rows, 2 * head_dim), shared_qk.dtype)] * 3
        + [pltpu.VMEM((2 * tok_rows, rows), jnp.float32)] * 2,
        scratch_shapes=[
            pltpu.VMEM(bucket_heads.shape, bucket_heads.dtype),
            *(own, own),
            pltpu.SemaphoreType.DMA((3,)),
            pltpu.SemaphoreType.DMA((FETCHES,)),
        ],
        compiler_params=vmem_params(12),
        name="attend_early",
    )(*(stays_in_hbm(array) for array in (bucket_heads, shared_qk, values, w_out)), *blocks)


def attend_kernel(*refs, bucket_count):
    refs, (late_score_ref, first_term_ref, second_term_ref) = refs[:-3], refs[-3:]
    query_rows, token_count = first_term_ref.shape
    tok_rows = query_rows // 2
    source_count = token_count // tok_rows
    pair_count = source_count // 2
    refs, (query_ref, key_ref, value_ref, *score_refs) = refs[:-5], refs[-5:]
    score_refs.append(late_score_ref)
    block_refs, out_refs = refs[5:-pair_count], refs[-pair_count:]
    head_dim = out_refs[0].shape[2]
    own = lax.axis_index("seq")
    owners = [(-step % pair_count, (own + flip) % 2) for step, flip in ((0, 0), *moves(source_count))]
    scale = 1.0 / math.sqrt(head_dim)
    strip = 16
    blocks = token_count // query_rows
    ahead = 2

    def scores_of(block, keys):
        queries = query_ref[block * query_rows : (block + 1) * query_rows, :]
        score_refs[block % 3][:, keys] = products(queries, key_ref[keys, :])

    def terms_of(score_ref, term_ref):
        for at in range(0, query_rows, strip):
            scores = score_ref[at : at + strip, :]
            row_max = jnp.max(scores, axis=1, keepdims=True)
            terms = jnp.exp2((scores - row_max) * (scale * math.log2(math.e)))
            term_ref[at : at + strip, :] = terms.astype(term_ref.dtype)

    def attend_of(block, term_ref):
        both = jnp.dot(term_ref[...], value_ref[...], preferred_element_type=jnp.float32)
        attended = (both[:, :head_dim] / both[:, head_dim:]).astype(out_refs[0].dtype)
        for at in range(0, query_rows, tok_rows):
            step, which = owners[(block * query_rows + at) // tok_rows]
            out_refs[step][which] = attended[at : at + tok_rows]

    for at, block_ref in enumerate(block_refs):
        stop = (source_count - len(block_refs) + at + 1) * tok_rows
        extend_received(block_ref, query_ref, key_ref, value_ref, slice(stop - tok_rows, stop), bucket_count)
        if stop % query_rows == 0:
            for block in range(ahead):
                scores_of(block, slice(stop - query_rows, stop))
    for block in range(blocks):
        if block + ahead < blocks:
            scores_of(block + ahead, slice(0, token_count))
            replace_diagonal(score_refs[(block + ahead) % 3], (block + ahead) * query_rows, tok_rows, head_dim)
        term_ref = (first_term_ref, second_term_ref)[block % 2]
        terms_of(score_refs[block % 3], term_ref)
        attend_of(block, term_ref)


def attend_head(early, blocks, bucket_count):
    token_count, head_dim = early[0].shape[0], early[0].shape[1] // 2
    tok_rows = early[-1].shape[0] // 2
    pair_count = token_count // (2 * tok_rows)
    dtype = early[0].dtype
    terms = pltpu.VMEM((2 * tok_rows, token_count), dtype)
    outs = pl.pallas_call(
        functools.partial(attend_kernel, bucket_count=bucket_count),
        in_specs=in_vmem(len(early) + len(blocks)),
        out_specs=in_vmem(pair_count + len(early)),
        out_shape=[pltpu.VMEM((2, tok_rows, head_dim), dtype)] * pair_count
        + [pltpu.VMEM(array.shape, array.dtype) for array in early],
        input_output_aliases={at: pair_count + at for at in range(len(early))},
        scratch_shapes=[pltpu.VMEM(early[-1].shape, early[-1].dtype), terms, terms],
        compiler_params=vmem_params(20),
        name="attend_head",
    )(*early, *blocks)
    return outs[:pair_count]


def fetch_kernel(w_hbm, after_ref, w_ref, sems):
    fetches = fetches_of(w_hbm, w_ref, w_hbm.shape[1] // 2 - w_ref.shape[1], sems)
    for fetch in fetches:
        fetch.start()
    for fetch in fetches:
        fetch.wait()


def fetch_theirs(w_out, after):
    return pl.pallas_call(
        fetch_kernel,
        in_specs=in_hbm(1) + in_vmem(1),
        out_specs=in_vmem(1)[0],
        out_shape=pltpu.VMEM((w_out.shape[0], w_out.shape[1] // 8 * 3), w_out.dtype),
        scratch_shapes=[pltpu.SemaphoreType.DMA((FETCHES,))],
        compiler_params=vmem_params(8),
        name="fetch_theirs",
    )(stays_in_hbm(w_out), after)


def gather_kernel(*refs):
    other = 1 - lax.axis_index("seq") % 2
    for at, pair_ref in enumerate(refs[:-1]):
        refs[-1][at] = pair_ref[other]


def gather_other(pairs):
    _, tok_rows, head_dim = pairs[0].shape
    return pl.pallas_call(
        gather_kernel,
        in_specs=in_vmem(len(pairs)),
        out_specs=in_vmem(1)[0],
        out_shape=pltpu.VMEM((len(pairs), tok_rows, head_dim), pairs[0].dtype),
        compiler_params=vmem_params(8),
        name="gather_other",
    )(*pairs)


def widen_kernel(*refs, pair_count):
    refs, (w_ref, out_ref, wide_ref) = refs[:-3], refs[-3:]
    pair_refs, swapped_refs = refs[:pair_count], refs[pair_count:]
    _, _, head_dim = pair_refs[0].shape
    swapped = [ref.at[at] for ref in swapped_refs for at in range(ref.shape[0])]
    own = lax.axis_index("seq")
    for step, pair_ref in enumerate(pair_refs):
        pair = (own // 2 + pair_count - step) % pair_count
        for rows, which in ((pair_ref[own % 2], own % 2), (swapped[step][...], 1 - own % 2)):
            start = pl.multiple_of((pair * 2 + which) * head_dim, head_dim)
            wide_ref[:, pl.ds(start, head_dim)] = rows
    out_ref[...] = jnp.dot(
        wide_ref[...], w_ref[:, : out_ref.shape[1]], preferred_element_type=jnp.float32
    ).astype(out_ref.dtype)


def widen_and_project(pairs, swapped, w_theirs, columns):
    tok_rows = pairs[0].shape[1]
    return pl.pallas_call(
        functools.partial(widen_kernel, pair_count=len(pairs)),
        in_specs=in_vmem(len(pairs) + len(swapped) + 1),
        out_specs=in_vmem(2),
        out_shape=[
            pltpu.VMEM((tok_rows, columns), w_theirs.dtype),
            pltpu.VMEM((tok_rows, w_theirs.shape[0]), w_theirs.dtype),
        ],
        compiler_params=vmem_params(16),
        name="widen_and_project",
    )(*pairs, *swapped, w_theirs)


def theirs_kernel(wide_ref, w_ref, out_ref, *, start):
    out_ref[...] = jnp.dot(
        wide_ref[...], w_ref[:, start : start + out_ref.shape[1]], preferred_element_type=jnp.float32
    ).astype(out_ref.dtype)


def project_theirs(wide, w_theirs, start):
    return pl.pallas_call(
        functools.partial(theirs_kernel, start=start),
        in_specs=in_vmem(2),
        out_specs=in_vmem(1)[0],
        out_shape=pltpu.VMEM((wide.shape[0], w_theirs.shape[1] - start), wide.dtype),
        compiler_params=vmem_params(16),
        name="project_theirs",
    )(wide, w_theirs)


def ours_kernel(wide_ref, w_hbm, out_ref, w_ref, sems):
    chunks, _, columns = w_ref.shape
    start = pl.multiple_of(lax.axis_index("mp") * (chunks * columns), columns)
    copies = [
        pltpu.make_async_copy(w_hbm.at[:, pl.ds(start + chunk * columns, columns)], w_ref.at[chunk], sems.at[chunk])
        for chunk in range(chunks)
    ]
    for copy in copies:
        copy.start()
    for chunk, copy in enumerate(copies):
        copy.wait()
        out_ref[:, chunk * columns : (chunk + 1) * columns] = jnp.dot(
            wide_ref[...], w_ref[chunk], preferred_element_type=jnp.float32
        )


def project_ours(wide, w_out):
    tok_rows, depth = wide.shape
    chunks = 4
    columns = w_out.shape[1] // (2 * chunks)
    return pl.pallas_call(
        ours_kernel,
        in_specs=in_vmem(1) + in_hbm(1),
        out_specs=in_vmem(1)[0],
        out_shape=pltpu.VMEM((tok_rows, chunks * columns), jnp.float32),
        scratch_shapes=[
            pltpu.VMEM((chunks, depth, columns), w_out.dtype),
            pltpu.SemaphoreType.DMA((chunks,)),
        ],
        compiler_params=vmem_params(20),
        name="project_ours",
    )(wide, stays_in_hbm(w_out))


def add_kernel(ours_ref, *refs):
    out_ref = refs[-1]
    start = 0
    for theirs_ref in refs[:-1]:
        at = slice(start, start + theirs_ref.shape[1])
        start = at.stop
        out_ref[:, at] = (ours_ref[:, at] + theirs_ref[...].astype(jnp.float32)).astype(out_ref.dtype)


def add_parts(ours, theirs, dtype):
    return pl.pallas_call(
        add_kernel,
        in_specs=in_vmem(1 + len(theirs)),
        out_shape=jax.ShapeDtypeStruct(ours.shape, dtype),
        compiler_params=vmem_params(8),
        name="add_parts",
    )(ours, *theirs)


def local_by_head(shared_qk, values, buckets, counts, w_out):
    bucket_heads = buckets.T
    seq_count = lax.axis_size("seq")
    received = [
        sent(block, step, flip)
        for (step, flip), block in zip(moves(seq_count), pack_blocks(bucket_heads, shared_qk, values))
    ]
    bucket_count = counts.shape[2]
    first_count = 2 * (5 * seq_count // 16) - 1
    w_first, *early = attend_early(bucket_heads, shared_qk, values, w_out, received[:first_count], bucket_count)
    pairs = list(attend_head(early, received[first_count:], bucket_count))
    w_rest = fetch_theirs(w_out, pairs[0])
    *others, last = pairs[1:]
    pairs = pairs[:1] + [sent(pair, step + 1, 0) for step, pair in enumerate(others)]
    pairs.append(sent(last, len(pairs), 0))
    cut = len(pairs) // 2 + 1
    swapped = [sent(gather_other(some), 0, 1) for some in (pairs[:cut], pairs[cut:])]
    first, wide = widen_and_project(pairs, swapped, w_first, w_first.shape[1])
    peers = [(0, 1), (1, 0)]
    arrived = [lax.ppermute(first, "mp", peers)]
    rest = project_theirs(wide, w_rest, 0)
    arrived.append(lax.ppermute(rest, "mp", peers))
    ours = project_ours(wide, w_out)
    return add_parts(ours, arrived, shared_qk.dtype)


def local(shared_qk, values, buckets, counts, w_out):
    head_count = buckets.shape[1]
    seq_count = lax.axis_size("seq")
    one_head_each = head_count == seq_count and counts.shape[2] == seq_count and 8 <= seq_count <= 128 and seq_count % 2 == 0
    if one_head_each and lax.axis_size("mp") == 2 and 2 * shared_qk.shape[0] <= BLOCK:
        return local_by_head(shared_qk, values, buckets, counts, w_out)
    return local_by_bucket(shared_qk, values, buckets, counts, w_out)


def solution(mesh):
    placed = (P("seq", "mp"), P("seq", "mp"), P("seq", "mp"), P(None, "mp", None), P("mp", None))
    return jax.shard_map(
        local, mesh=mesh, in_specs=placed, out_specs=P("seq", "mp"), check_vma=False
    )
```
